128 devices in a mesh: row: 16 (over z_lo, y, core), col: 8 (over z_hi, x).
Axes of the slice: x: 4, y: 4, z: 4 (z_hi: 2, z_lo: 2; z = z_hi * 2 + z_lo), core: 2. Of those that a mesh axis runs over, the one named last changes fastest.
Arguments:
- hidden: bfloat16 [6144, 5120], P('row', 'col'), may hold values from -6 to 6
- modulation: float32 [2, 5120], replicated, may hold values from -3 to 3
- w_query: bfloat16 [5120, 5120], P('row', 'col'), may hold values from -2 to 2
- w_key: bfloat16 [5120, 5120], P('row', 'col'), may hold values from -2 to 2
- w_value: bfloat16 [5120, 5120], P('row', 'col'), may hold values from -0.078125 to 0.078125
- q_gain: float32 [5120], P('col'), may hold values from 0.4 to 4.3
- k_gain: float32 [5120], P('col'), may hold values from 0.4 to 4.3
- positions: int32 [3, 6144], P(None, 'row'), may hold values from 0 to 63
- segment_ids: int32 [6144], replicated, may hold values from 0 to 11, never falling along the last dimension, each value on 1 to 3072 neighbouring positions
- page_table: int32 [48], replicated, may hold values from 0 to 47, each once
Outputs:
- attended: bfloat16 [6144, 5120], P('row', 'col')
- page_store: bfloat16 [2, 48, 128, 5120], P(None, 'row', None, 'col')
The draws below stay inside these ranges and needn't reach their ends.
Inputs may be any that keep to these rules, and one draw needn't show every extreme that they name: `segment_ids`: segment numbers never fall along the tokens; each segment holds at most 3072 tokens, and one holds exactly 3072. `page_table`: every slot is named by exactly one block.
All inputs are finite; a program needn't handle non-finite values.
Results may differ from the reference program's by a relative error of at most 0.015.
Values may be sent and summed in bfloat16 or wider, within the bound.
A program may use at most 128 MiB of HBM per device.

```python
import math
import jax
import jax.numpy as jnp
import numpy as np
from jax import lax

D = 5120
HEADS = 40
HEAD_DIM = 128
PAGE = 128
SEGS = 12
TOKENS = 6144
MOST = 3072
PAGES = 48
FEAT_BLK = 320


def column_scale(key):
    fraction = jnp.arange(D, dtype=jnp.float32) / (D - 1)
    spread = jax.random.uniform(key, (D,), jnp.float32, 0.0, math.log(4.0))
    return jnp.exp(math.log(3.0) * fraction + spread)


def draw_w_query(key, part):
    shared = jax.random.normal(jax.random.fold_in(key, 1), (D, D), jnp.float32)
    return (shared * D ** (-0.5) * column_scale(jax.random.fold_in(key, 3))).astype(jnp.bfloat16)


def draw_w_key(key, part):
    separate = jax.random.normal(jax.random.fold_in(key, 2), (D, D), jnp.float32)
    mixture = separate
    scaled = column_scale(jax.random.fold_in(key, 4))
    return (mixture * D ** (-0.5) * scaled).astype(jnp.bfloat16)


def gain_draw(key):
    jitter = jax.random.uniform(jax.random.fold_in(key, 5), (D,), jnp.float32, 0.6, 1.6)
    return jitter


def draw_q_gain(key, part):
    return gain_draw(jax.random.fold_in(key, 21))


def draw_k_gain(key, part):
    return gain_draw(jax.random.fold_in(key, 22))


def plant(result, rng, smallest, high):
    longest = result.shape.index(max(result.shape))
    spots = []
    for shift in (0, 1):
        where = [jax.random.randint(jax.random.fold_in(rng, axis), (), 0, length) for axis, length in enumerate(result.shape)]
        where[longest] = (where[longest] + shift) % result.shape[longest]
        spots.append(tuple(where))
    return result.at[spots[0]].set(smallest).at[spots[1]].set(high)


def shard_levels(key, dims, pieces, low, top_value):
    factor_of = 1.0
    for axis_at, parts in pieces:
        draws = jax.random.uniform(jax.random.fold_in(jax.random.fold_in(key, 6), axis_at), (parts,), jnp.float32, low / len(pieces), top_value / len(pieces))
        factor_of = factor_of * jnp.repeat(jnp.exp(draws), dims[axis_at] // parts).reshape((-1,) + (1,) * (len(dims) - 1 - axis_at))
    return factor_of


def length_profile(amount, total, reach, skew):
    portions = [(1 << 20) // math.isqrt(grade ** skew) + 1 for grade in range(2, amount + 1)]
    surplus, holding = total - reach - (amount - 1), [1] * (amount - 1)
    while surplus > 0:
        candidates = [i for i in range(amount - 1) if holding[i] < reach]
        whole, budget = sum([portions[i] for i in candidates]), surplus
        for i in candidates:
            more = min(reach - holding[i], max(1, budget * portions[i] // whole), surplus)
            holding[i] = holding[i] + more
            surplus = surplus - more
    return np.array([reach] + holding)


def uneven(stream_key, count, total, most, lean):
    if count == 2:
        one = jax.random.randint(stream_key, (), max(1, total - most), min(most, total - 1) + 1)
        return jnp.stack([one, total - one])
    lengths = jnp.asarray(length_profile(count, total, most, lean), jnp.int32)
    pairs = (count - 1) // 2
    giver, sink = lengths[1:1 + 2 * pairs:2], lengths[2:2 + 2 * pairs:2]
    room = jnp.minimum(giver - 1, most - sink)
    passed = jax.random.randint(jax.random.fold_in(stream_key, 1), (pairs,), 0, 1 << 20) % (room + 1)
    lengths = lengths.at[1:1 + 2 * pairs:2].set(giver - passed).at[2:2 + 2 * pairs:2].set(sink + passed)
    return lengths[jax.random.permutation(jax.random.fold_in(stream_key, 2), count)]


def scatter_about(rng, dims, scale, reach, split=(), kind=jnp.bfloat16):
    loudness = shard_levels(rng, dims, split, -0.22, 0.18) if split else 1.0
    array = jax.random.normal(rng, dims, jnp.float32) * scale * loudness
    return jnp.minimum(jnp.maximum(array, -reach), reach).astype(kind)


def setup_inputs(seed: int = 0) -> dict:
    keys = jax.random.split(jax.random.key(seed), 11)
    hidden = scatter_about(keys[0], (TOKENS, D), 1.0, 6.0, ((0, 16), (1, 8)))
    modulation = scatter_about(keys[1], (2, D), 0.5, 3.0, (), jnp.float32)
    w_query = draw_w_query(jax.random.fold_in(keys[10], 71), 0)
    w_key = draw_w_key(jax.random.fold_in(keys[10], 71), 0)
    w_value = scatter_about(keys[4], (D, D), D ** -0.5, 0.078125, ((0, 16), (1, 8)))
    q_gain = draw_q_gain(jax.random.fold_in(keys[10], 71), 0)
    k_gain = draw_k_gain(jax.random.fold_in(keys[10], 71), 0)
    positions = plant(jax.random.randint(keys[7], (3, TOKENS), 0, 64), jax.random.fold_in(keys[7], 1), 0, 63).astype(jnp.int32)
    segment_ids = jnp.searchsorted(jnp.cumsum(uneven(keys[8], SEGS, TOKENS, MOST, 2)), jnp.arange(TOKENS), side="right").astype(jnp.int32)
    page_table = jax.random.permutation(keys[9], PAGES).astype(jnp.int32)
    return dict(hidden=hidden, modulation=modulation, w_query=w_query, w_key=w_key, w_value=w_value, q_gain=q_gain, k_gain=k_gain, positions=positions, segment_ids=segment_ids, page_table=page_table)


epsilon = 1e-06

def rotary_table(positions, pair_count):
    frame_pairs = pair_count - 2 * (pair_count // 3)
    side_pairs = pair_count // 3
    column = jnp.arange(pair_count)
    frame_rate = 10000.0 ** (-column.astype(jnp.float32) / frame_pairs)
    height_rate = 10000.0 ** (-(column - frame_pairs).astype(jnp.float32) / side_pairs)
    width_rate = 10000.0 ** (-(column - frame_pairs - side_pairs).astype(jnp.float32) / side_pairs)
    coords = positions.astype(jnp.float32)
    angles = jnp.where(column < frame_pairs, coords[0][:, None] * frame_rate, jnp.where(column < frame_pairs + side_pairs, coords[1][:, None] * height_rate, coords[2][:, None] * width_rate))
    return (jnp.cos(angles), jnp.sin(angles))

def rotate(values, cosine, sine_table, head_dim):
    row_count = values.shape[0]
    head_count = values.shape[1] // head_dim
    paired = values.reshape(row_count, head_count, head_dim // 2, 2)
    former = paired[..., 0]
    latter = paired[..., 1]
    cosine = cosine[:, None, :]
    sine_table = sine_table[:, None, :]
    turned = jnp.stack([former * cosine - latter * sine_table, former * sine_table + latter * cosine], axis=-1)
    return turned.reshape(row_count, head_count * head_dim)

def modulate(activations, modulation):
    average = lax.optimization_barrier(jnp.mean(activations, axis=1, keepdims=True))
    centred = activations - average
    variance = lax.optimization_barrier(jnp.mean(centred * centred, axis=1, keepdims=True))
    normed = centred * lax.rsqrt(variance + epsilon)
    return (normed * (1.0 + modulation[1]) + modulation[0]).astype(jnp.bfloat16)

def project(modulated, weight):

    def add_block(summed, block_number):
        columns = lax.dynamic_slice_in_dim(modulated, block_number * FEAT_BLK, FEAT_BLK, 1)
        weight_rows = lax.dynamic_slice_in_dim(weight, block_number * FEAT_BLK, FEAT_BLK, 0)
        partial_value = jnp.dot(columns, weight_rows, preferred_element_type=jnp.float32).astype(jnp.bfloat16)
        partial_value = lax.optimization_barrier(partial_value)
        return (summed + partial_value.astype(jnp.float32), None)
    starting = jnp.zeros((modulated.shape[0], weight.shape[1]), jnp.float32)
    summed, _ = lax.scan(add_block, starting, jnp.arange(D // FEAT_BLK, dtype=jnp.int32))
    return summed

def reference(hidden, modulation, w_query, w_key, w_value, q_gain, k_gain, positions, segment_ids, page_table):
    modulated = modulate(hidden.astype(jnp.float32), modulation)
    query_raw = project(modulated, w_query)
    key_raw = project(modulated, w_key)
    value_raw = project(modulated, w_value)
    query_normed = query_raw * lax.rsqrt(lax.optimization_barrier(jnp.mean(query_raw * query_raw, axis=1, keepdims=True)) + epsilon) * q_gain
    key_normed = key_raw * lax.rsqrt(lax.optimization_barrier(jnp.mean(key_raw * key_raw, axis=1, keepdims=True)) + epsilon) * k_gain
    cosine, sine_table = rotary_table(positions, HEAD_DIM // 2)
    query = rotate(query_normed, cosine, sine_table, HEAD_DIM).astype(jnp.bfloat16)
    key = rotate(key_normed, cosine, sine_table, HEAD_DIM).astype(jnp.bfloat16)
    value = value_raw.astype(jnp.bfloat16)
    heads_query = query.reshape(TOKENS, HEADS, HEAD_DIM).transpose(1, 0, 2)
    heads_key = key.reshape(TOKENS, HEADS, HEAD_DIM).transpose(1, 0, 2)
    heads_value = value.reshape(TOKENS, HEADS, HEAD_DIM).transpose(1, 0, 2)
    allowed = segment_ids[:, None] == segment_ids[None, :]

    def one_head(operands):
        head_query, head_key, head_value = operands
        scores = jnp.dot(head_query, head_key.T, preferred_element_type=jnp.float32) * HEAD_DIM ** (-0.5)
        highest = lax.optimization_barrier(jnp.max(jnp.where(allowed, scores, -1e+30), axis=1, keepdims=True))
        probabilities = jnp.where(allowed, jnp.exp(scores - highest), 0.0)
        summed = lax.optimization_barrier(jnp.sum(probabilities, axis=1, keepdims=True))
        mixed = jnp.dot(probabilities.astype(jnp.bfloat16), head_value, preferred_element_type=jnp.float32)
        return mixed / summed
    outputs = lax.map(one_head, (heads_query, heads_key, heads_value))
    attended = outputs.transpose(1, 0, 2).reshape(TOKENS, D).astype(jnp.bfloat16)
    paged = jnp.stack([key, value]).reshape(2, PAGES, PAGE, D)
    page_store = jnp.zeros_like(paged).at[:, page_table].set(paged)
    return (attended, page_store)
```

```python
import functools

import jax
import jax.numpy as jnp
from jax import lax
from jax.experimental import pallas as pl
from jax.experimental.pallas import tpu as pltpu
from jax.sharding import PartitionSpec as P

HEAD_DIM = 128
PAGE = 128
KEY_BLOCK = 512
LOG2E = 1.4426950408889634
epsilon = 1e-06


def rotary_table(positions, pair_count):
    frame_pairs = pair_count - 2 * (pair_count // 3)
    side_pairs = pair_count // 3
    column = jnp.arange(pair_count)
    frame_rate = 10000.0 ** (-column.astype(jnp.float32) / frame_pairs)
    height_rate = 10000.0 ** (-(column - frame_pairs).astype(jnp.float32) / side_pairs)
    width_rate = 10000.0 ** (-(column - frame_pairs - side_pairs).astype(jnp.float32) / side_pairs)
    coords = positions.astype(jnp.float32)
    angles = jnp.where(
        column < frame_pairs,
        coords[0][:, None] * frame_rate,
        jnp.where(
            column < frame_pairs + side_pairs,
            coords[1][:, None] * height_rate,
            coords[2][:, None] * width_rate,
        ),
    )
    return (jnp.cos(angles), jnp.sin(angles))


def rotate(values, cosine, sine_table, head_dim):
    row_count = values.shape[0]
    head_count = values.shape[1] // head_dim
    paired = values.reshape(row_count, head_count, head_dim // 2, 2)
    former = paired[..., 0]
    latter = paired[..., 1]
    cosine = cosine[:, None, :]
    sine_table = sine_table[:, None, :]
    turned = jnp.stack(
        [former * cosine - latter * sine_table, former * sine_table + latter * cosine], axis=-1
    )
    return turned.reshape(row_count, head_count * head_dim)


def modulate(activations, modulation):
    average = jnp.mean(activations, axis=1, keepdims=True)
    centred = activations - average
    variance = jnp.mean(centred * centred, axis=1, keepdims=True)
    normed = centred * lax.rsqrt(variance + epsilon)
    return (normed * (1.0 + modulation[1]) + modulation[0]).astype(jnp.bfloat16)


def attend_kernel(
    plan, query, keys, values, query_segs, key_segs, attended, pages,
    key_buf, value_buf, top, acc, load_sem, page_sem,
):
    rows, width = query.shape
    heads = width // HEAD_DIM
    block = KEY_BLOCK
    own_pages = pages.shape[1]
    lo, hi = plan[0], plan[1]

    def page_copy(which, j):
        source = (keys, values)[which]
        start = pl.multiple_of(plan[2 + j] * PAGE, PAGE)
        return pltpu.make_async_copy(
            source.at[pl.ds(start, PAGE)], pages.at[which, j], page_sem.at[which, j]
        )

    def load(number, slot):
        start = pl.multiple_of(number * block, block)
        return (
            pltpu.make_async_copy(
                keys.at[pl.ds(start, block)], key_buf.at[slot], load_sem.at[0, slot]
            ),
            pltpu.make_async_copy(
                values.at[pl.ds(start, block)], value_buf.at[slot], load_sem.at[1, slot]
            ),
        )

    for copy in load(lo, 0):
        copy.start()
    for which in range(2):
        for j in range(own_pages):
            page_copy(which, j).start()
    top[...] = jnp.full_like(top, -1e30)
    acc[...] = jnp.zeros_like(acc)
    ones = jnp.ones((block, HEAD_DIM), jnp.bfloat16)
    scale = HEAD_DIM ** (-0.5) * LOG2E

    @pl.loop(lo, hi)
    def _(number):
        slot = lax.rem(number - lo, 2)
        for copy in load(number, slot):
            copy.wait()

        @pl.when(number + 1 < hi)
        def _():
            for copy in load(number + 1, 1 - slot):
                copy.start()

        allowed = query_segs[:, 0:1] == key_segs[number]
        for h in range(heads):
            part = pl.ds(h * HEAD_DIM, HEAD_DIM)
            scores = lax.dot_general(
                query[:, part], key_buf[slot, :, part], (((1,), (1,)), ((), ())),
                preferred_element_type=jnp.float32,
            ) * scale
            scores = jnp.where(allowed, scores, -1e30)
            old = top[h]
            new = jnp.maximum(old, jnp.max(scores, axis=1, keepdims=True))
            top[h] = new
            weights = jnp.where(allowed, jnp.exp2(scores - new[:, 0:1]), 0.0)
            factor = jnp.exp2(old - new)
            mixed = jnp.dot(
                weights.astype(jnp.bfloat16),
                jnp.concatenate([value_buf[slot, :, part], ones], axis=1),
                preferred_element_type=jnp.float32,
            )
            acc[h] = acc[h] * jnp.concatenate([factor, factor], axis=1) + mixed

    for h in range(heads):
        part = pl.ds(h * HEAD_DIM, HEAD_DIM)
        attended[:, part] = (acc[h, :, :HEAD_DIM] / acc[h, :, HEAD_DIM:]).astype(attended.dtype)
    for which in range(2):
        for j in range(own_pages):
            page_copy(which, j).wait()


def attend(query, keys, values, segment_ids, page_table):
    rows, width = query.shape
    heads = width // HEAD_DIM
    tokens = keys.shape[0]
    row = lax.axis_index("row")
    query_segs = lax.dynamic_slice_in_dim(segment_ids, row * rows, rows, 0)
    first, last = query_segs[0], query_segs[-1]
    lo = jnp.sum(segment_ids < first) // KEY_BLOCK
    hi = (jnp.sum(segment_ids <= last) + KEY_BLOCK - 1) // KEY_BLOCK
    own_pages = rows // PAGE
    slots = row * own_pages + jnp.arange(own_pages)
    numbers = jnp.arange(page_table.shape[0], dtype=jnp.int32)
    owned = jnp.sum(jnp.where(page_table[None] == slots[:, None], numbers[None], 0), axis=1)
    plan = jnp.concatenate([jnp.stack([lo, hi]).astype(jnp.int32), owned.astype(jnp.int32)])
    any_spec = pl.BlockSpec(memory_space=pl.ANY)
    vmem = pl.BlockSpec(memory_space=pltpu.VMEM)
    return pl.pallas_call(
        attend_kernel,
        out_shape=(
            jax.ShapeDtypeStruct((rows, width), jnp.bfloat16),
            jax.ShapeDtypeStruct((2, own_pages, PAGE, width), jnp.bfloat16),
        ),
        in_specs=[
            pl.BlockSpec(memory_space=pltpu.SMEM), vmem, any_spec, any_spec, vmem, vmem,
        ],
        out_specs=(vmem, any_spec),
        scratch_shapes=[
            pltpu.VMEM((2, KEY_BLOCK, width), jnp.bfloat16),
            pltpu.VMEM((2, KEY_BLOCK, width), jnp.bfloat16),
            pltpu.VMEM((heads, rows, HEAD_DIM), jnp.float32),
            pltpu.VMEM((heads, rows, 2 * HEAD_DIM), jnp.float32),
            pltpu.SemaphoreType.DMA((2, 2)),
            pltpu.SemaphoreType.DMA((2, own_pages)),
        ],
        compiler_params=pltpu.CompilerParams(vmem_limit_bytes=40 * 2**20),
        name="attend",
    )(
        plan, query, keys, values, query_segs[:, None],
        segment_ids.reshape(tokens // KEY_BLOCK, 1, KEY_BLOCK),
    )


def body(
    hidden, modulation, w_query, w_key, w_value, q_gain, k_gain, positions, segment_ids, page_table
):
    w_query, w_key, w_value = (
        lax.all_gather(w, "row", axis=0, tiled=True) for w in (w_query, w_key, w_value)
    )
    full_rows = lax.all_gather(hidden, "col", axis=1, tiled=True)
    modulated = modulate(full_rows.astype(jnp.float32), modulation)
    full_width = full_rows.shape[1]
    query_raw, key_raw, value_raw = (
        jnp.dot(modulated, w, preferred_element_type=jnp.float32)
        for w in (w_query, w_key, w_value)
    )
    squares = lax.psum(
        (jnp.sum(query_raw * query_raw, axis=1), jnp.sum(key_raw * key_raw, axis=1)), "col"
    )
    query_normed = query_raw * lax.rsqrt(squares[0][:, None] / full_width + epsilon) * q_gain
    key_normed = key_raw * lax.rsqrt(squares[1][:, None] / full_width + epsilon) * k_gain
    cosine, sine_table = rotary_table(positions, HEAD_DIM // 2)
    query = rotate(query_normed, cosine, sine_table, HEAD_DIM).astype(jnp.bfloat16)
    key = rotate(key_normed, cosine, sine_table, HEAD_DIM).astype(jnp.bfloat16)
    value = value_raw.astype(jnp.bfloat16)
    keys_all = lax.all_gather(key, "row", axis=0, tiled=True)
    values_all = lax.all_gather(value, "row", axis=0, tiled=True)
    return attend(query, keys_all, values_all, segment_ids, page_table)


def solution(mesh):
    in_specs = (
        P("row", "col"),
        P(),
        P("row", "col"),
        P("row", "col"),
        P("row", "col"),
        P("col"),
        P("col"),
        P(None, "row"),
        P(),
        P(),
    )
    out_specs = (P("row", "col"), P(None, "row", None, "col"))
    return jax.shard_map(body, mesh=mesh, in_specs=in_specs, out_specs=out_specs, check_vma=False)
```

```python
import jax
import jax.numpy as jnp
import numpy as np
from jax import lax
from jax.experimental import pallas as pl
from jax.experimental.pallas import tpu as pltpu
from jax.sharding import PartitionSpec as P

HEAD_DIM = 128
PAGE = 128
KEY_BLOCK = 512
LOG2E = 1.4426950408889634
epsilon = 1e-06


def rotary_rates(pair_count):
    frame_pairs = pair_count - 2 * (pair_count // 3)
    side_pairs = pair_count // 3
    column = np.arange(pair_count)
    starts = [0, frame_pairs, frame_pairs + side_pairs, pair_count]
    rates = np.zeros((8, 2 * pair_count), np.float32)
    for i in range(3):
        count = starts[i + 1] - starts[i]
        rate = np.power(10000.0, -(column - starts[i]) / count).astype(np.float32)
        inside = (column >= starts[i]) & (column < starts[i + 1])
        rates[i] = np.repeat(np.where(inside, rate, 0.0), 2)
    return rates


class Ring:
    def __init__(self, net, name, own, buffer, pair_first, sibling):
        self.net, self.name, self.own, self.buffer = net, name, own, buffer
        self.pair_first, self.sibling = pair_first, sibling

    def view(self, pair, step, half=None, other=False):
        return self.buffer(self.net.slot(self.name, pair, step, other), half)

    def put(self, source, target, kind, link):
        self.net.put(source, target, (self.name, kind), self.net.device(self.name, link))

    def got(self, kind, view):
        self.net.got(view, (self.name, kind))

    def start(self):
        mine = self.view(0, 0)
        if self.pair_first:
            self.put(self.own, mine, "p", "pair")
        self.put(self.own, mine, "m", "up")
        self.put(self.own, mine, "n", "down")
        if not self.pair_first:
            self.put(self.own, mine, "p", "pair")
        if self.sibling:
            self.put(self.own, mine, "so", "core")
        self.net.local(self.own, mine)

    def share(self, kind, view):
        if self.sibling:
            self.put(view, view, "s" + kind, "core")

    def events(self):
        def pair():
            view = self.view(1, 0)
            self.got("p", view)
            if self.pair_first:
                self.put(view, view, "pm", "up")
                self.put(view, view, "pn", "down")
            self.share("p", view)

        def ring(prefix, where, direction):
            def run():
                step, kind, half, link = (
                    (-1, "m", 0, "up") if direction == 0 else (1, "n", 1, "down")
                )
                view = self.view(where, step)
                self.got(prefix + kind, view)
                if where == 0 or self.pair_first:
                    part = self.view(where, step, half)
                    self.put(part, part, prefix + ("a", "b")[direction], link)
                if where == 0 and not self.pair_first:
                    self.put(view, view, "p" + kind, "pair")
                self.share(prefix + kind, view)

            return run

        def far(prefix, where):
            def run():
                view = self.view(where, 2)
                if where == 0 or self.pair_first:
                    for half, kind in enumerate("ab"):
                        self.got(prefix + kind, self.view(where, 2, half))
                else:
                    self.got(prefix + "f", view)
                if where == 0 and not self.pair_first:
                    self.put(view, view, "pf", "pair")
                self.share(prefix + "f", view)

            return run

        near = [ring("", 0, 0), ring("", 0, 1)]
        crossed = [ring("p", 1, 0), ring("p", 1, 1)]
        if self.pair_first:
            return [pair, *near, *crossed, far("", 0), far("p", 1)]
        return [*near, pair, far("", 0), *crossed, far("p", 1)]

    def finish(self):
        if self.sibling:
            self.got("so", self.view(0, 0, other=True))
            for prefix, where in (("", 0), ("p", 1)):
                self.got("s" + prefix + "m", self.view(where, -1, other=True))
                self.got("s" + prefix + "n", self.view(where, 1, other=True))
                self.got("s" + prefix + "f", self.view(where, 2, other=True))
            self.got("sp", self.view(1, 0, other=True))


class Net:
    def __init__(self, send, recv, own_sem):
        self.send, self.recv, self.own_sem = send, recv, own_sem
        self.sent, self.kinds, self.locals = [], {}, []
        row, col = lax.axis_index("row"), lax.axis_index("col")
        self.row, self.col = row, col
        self.core, self.y, self.z_lo = row % 2, (row // 2) % 4, row // 8
        self.x, self.z_hi = col % 4, col // 4

    def row_at(self, pair, step, other):
        z_lo = 1 - self.z_lo if pair else self.z_lo
        core = 1 - self.core if other else self.core
        return z_lo * 8 + ((self.y + step + 4) % 4) * 2 + core

    def col_at(self, pair, step):
        z_hi = 1 - self.z_hi if pair else self.z_hi
        return z_hi * 4 + (self.x + step + 4) % 4

    def slot(self, name, pair, step, other):
        return self.col_at(pair, step) if name == "x" else self.row_at(pair, step, other)

    def device(self, name, link):
        pair, step = {"pair": (1, 0), "up": (0, 1), "down": (0, -1), "core": (0, 0)}[link]
        if name == "x":
            return (self.row, self.col_at(pair, step))
        return (self.row_at(pair, step, link == "core"), self.col)

    def partners(self):
        rows = [self.device("w", link) for link in ("pair", "up", "down", "core")]
        return rows + self.peers()

    def peers(self):
        others = [(p, s) for p in (0, 1) for s in range(4) if (p, s) != (0, 0)]
        return [(self.row, self.col_at(*o)) for o in others]

    def number(self, kind):
        return self.kinds.setdefault(kind, len(self.kinds))

    def copy(self, source, target, kind, device):
        return pltpu.make_async_remote_copy(
            src_ref=source,
            dst_ref=target,
            send_sem=self.send.at[len(self.sent)],
            recv_sem=self.recv.at[self.number(kind)],
            device_id=device,
            device_id_type=pl.DeviceIdType.MESH,
        )

    def put(self, source, target, kind, device):
        copy = self.copy(source, target, kind, device)
        copy.start()
        self.sent.append(copy)

    def got(self, view, kind):
        pltpu.make_async_remote_copy(
            src_ref=view,
            dst_ref=view,
            send_sem=self.send.at[0],
            recv_sem=self.recv.at[self.number(kind)],
            device_id=self.device("w", "core"),
            device_id_type=pl.DeviceIdType.MESH,
        ).wait_recv()

    def local(self, source, target):
        copy = pltpu.make_async_copy(source, target, self.own_sem.at[len(self.locals)])
        copy.start()
        self.locals.append(copy)


def project_kernel(
    hidden, modulation, w_query, w_key, w_value, q_gain, k_gain, places, rates,
    query_out, keys_all, values_all,
    hidden_all, modulated, weights, raw, key_own, value_own, squares, tables,
    send, recv, own_sem,
):
    net = Net(send, recv, own_sem)
    rows, width = hidden.shape
    deep = w_query.shape[0]
    features = modulation.shape[1]
    heads = width // HEAD_DIM

    barrier = pltpu.get_barrier_semaphore()
    partners = net.partners()
    for device in partners:
        pl.semaphore_signal(
            barrier, inc=1, device_id=device, device_id_type=pl.DeviceIdType.MESH
        )
    pl.semaphore_wait(barrier, len(partners))

    def cut(start, size, half):
        if half is None:
            return pl.ds(pl.multiple_of(start, 16), size)
        return pl.ds(pl.multiple_of(start + half * (size // 2), 16), size // 2)

    def weight_view(which):
        return lambda slot, half: weights.at[which, cut(slot * deep, deep, half)]

    def token_view(ref):
        return lambda slot, half: ref.at[slot, cut(0, rows, half)]

    hid = Ring(net, "x", hidden, token_view(hidden_all), True, False)
    wk = Ring(net, "wk", w_key, weight_view(1), True, True)
    wv = Ring(net, "wv", w_value, weight_view(2), False, True)
    wq = Ring(net, "wq", w_query, weight_view(0), True, True)
    kk = Ring(net, "kk", key_own, token_view(keys_all), True, True)
    vv = Ring(net, "vv", value_own, token_view(values_all), False, True)

    def pull(*queues):
        queues = [list(q) for q in queues]
        while any(queues):
            for q in queues:
                if q:
                    q.pop(0)()

    hid.start()
    wv.start()
    wk.start()

    angle = (
        places[:, 0:1] * rates[0:1] + places[:, 1:2] * rates[1:2] + places[:, 2:3] * rates[2:3]
    )
    lane = lax.broadcasted_iota(jnp.int32, angle.shape, 1)
    even = lane % 2 == 0
    tables[0] = jnp.cos(angle)
    sine = jnp.sin(angle)
    tables[1] = jnp.where(even, -sine, sine)

    def normalise():
        net.locals[0].wait()
        groups = hidden_all.shape[0]

        def add(g, total):
            return total + jnp.sum(hidden_all[g].astype(jnp.float32), axis=1, keepdims=True)

        zero = jnp.zeros((rows, 1), jnp.float32)
        average = lax.fori_loop(0, groups, add, zero) / features

        def spread(g, total):
            centred = hidden_all[g].astype(jnp.float32) - average
            return total + jnp.sum(centred * centred, axis=1, keepdims=True)

        variance = lax.fori_loop(0, groups, spread, zero) / features
        scale = lax.rsqrt(variance + epsilon)

        @pl.loop(0, groups)
        def _(g):
            part = pl.ds(pl.multiple_of(g * width, width), width)
            normed = (hidden_all[g].astype(jnp.float32) - average) * scale
            shifted = normed * (1.0 + modulation[1:2, part]) + modulation[0:1, part]
            modulated[:, part] = shifted.astype(jnp.bfloat16)

    def project(which):
        step = 2 * width
        raw[...] = jnp.zeros_like(raw)

        @pl.loop(0, features // step)
        def _(g):
            part = pl.ds(pl.multiple_of(g * step, step), step)
            raw[...] += jnp.dot(
                modulated[:, part], weights[which, part, :], preferred_element_type=jnp.float32
            )

    def send_squares(number):
        whole = raw[...]
        part = jnp.zeros((rows, HEAD_DIM), jnp.float32)
        for h in range(heads):
            piece = whole[:, h * HEAD_DIM : (h + 1) * HEAD_DIM]
            part = part + piece * piece
        total = jnp.sum(part.T, axis=0, keepdims=True)
        mine = squares.at[number, net.col]
        squares[number, net.col] = jnp.broadcast_to(total, (8, rows))
        for i, device in enumerate(net.peers()):
            net.put(mine, mine, ("sq", number, i), device)

    def turned(number, gain):
        others = [(p, s) for p in (0, 1) for s in range(4) if (p, s) != (0, 0)]
        for i, (pair, step) in enumerate(others):
            net.got(squares.at[number, net.col_at(pair, -step)], ("sq", number, i))
        total = jnp.sum(squares[number], axis=0)
        column = jnp.broadcast_to(total[0:1], (HEAD_DIM, rows)).T
        factor = lax.rsqrt(column / features + epsilon)
        made = []
        for h in range(heads):
            part = slice(h * HEAD_DIM, (h + 1) * HEAD_DIM)
            normed = raw[:, part] * factor * gain[0:1, part]
            swapped = jnp.where(
                even, pltpu.roll(normed, HEAD_DIM - 1, 1), pltpu.roll(normed, 1, 1)
            )
            made.append((normed * tables[0] + swapped * tables[1]).astype(jnp.bfloat16))
        return jnp.concatenate(made, axis=1)

    pull(wv.events(), wk.events(), hid.events())
    wq.start()
    normalise()
    wv.finish()
    for copy in net.locals[1:3]:
        copy.wait()
    project(2)
    value_own[...] = raw[...].astype(jnp.bfloat16)
    vv.start()
    wk.finish()
    project(1)
    send_squares(0)
    queue = wq.events()
    for event in queue[:3]:
        event()
    key_own[...] = turned(0, k_gain)
    kk.start()
    pull(queue[3:], vv.events(), kk.events())
    wq.finish()
    net.locals[3].wait()
    project(0)
    send_squares(1)
    query_out[...] = turned(1, q_gain)
    vv.finish()
    kk.finish()
    for copy in net.locals[4:]:
        copy.wait()
    for copy in net.sent:
        copy.wait_send()


def project(hidden, modulation, w_query, w_key, w_value, q_gain, k_gain, positions):
    rows, width = hidden.shape
    deep = w_query.shape[0]
    features = modulation.shape[1]
    members, groups = features // deep, features // width
    places = positions.astype(jnp.float32).T
    any_spec = pl.BlockSpec(memory_space=pl.ANY)
    vmem = pl.BlockSpec(memory_space=pltpu.VMEM)
    tokens = jax.ShapeDtypeStruct((members, rows, width), jnp.bfloat16)
    return pl.pallas_call(
        project_kernel,
        out_shape=(jax.ShapeDtypeStruct((rows, width), jnp.bfloat16), tokens, tokens),
        in_specs=[vmem, vmem, any_spec, any_spec, any_spec, vmem, vmem, vmem, vmem],
        out_specs=(vmem, any_spec, any_spec),
        scratch_shapes=[
            pltpu.VMEM((groups, rows, width), jnp.bfloat16),
            pltpu.VMEM((rows, features), jnp.bfloat16),
            pltpu.VMEM((3, features, width), jnp.bfloat16),
            pltpu.VMEM((rows, width), jnp.float32),
            pltpu.VMEM((rows, width), jnp.bfloat16),
            pltpu.VMEM((rows, width), jnp.bfloat16),
            pltpu.VMEM((2, groups, 8, rows), jnp.float32),
            pltpu.VMEM((2, rows, HEAD_DIM), jnp.float32),
            pltpu.SemaphoreType.DMA((128,)),
            pltpu.SemaphoreType.DMA((128,)),
            pltpu.SemaphoreType.DMA((6,)),
        ],
        compiler_params=pltpu.CompilerParams(
            collective_id=0, has_side_effects=True, vmem_limit_bytes=56 * 2**20
        ),
        name="project",
    )(
        hidden, modulation, w_query, w_key, w_value, q_gain[None], k_gain[None], places,
        jnp.asarray(rotary_rates(HEAD_DIM // 2)),
    )


def attend_kernel(
    plan, query, keys, values, query_segs, key_segs, attended, pages,
    key_buf, value_buf, top, acc, load_sem, page_sem,
):
    rows, width = query.shape
    heads = width // HEAD_DIM
    block = KEY_BLOCK
    own_pages = pages.shape[1]
    lo, hi = plan[0], plan[1]

    def page_copy(which, j):
        source = (keys, values)[which]
        start = pl.multiple_of(plan[2 + j] * PAGE, PAGE)
        return pltpu.make_async_copy(
            source.at[pl.ds(start, PAGE)], pages.at[which, j], page_sem.at[which, j]
        )

    def load(number, slot):
        start = pl.multiple_of(number * block, block)
        return (
            pltpu.make_async_copy(
                keys.at[pl.ds(start, block)], key_buf.at[slot], load_sem.at[0, slot]
            ),
            pltpu.make_async_copy(
                values.at[pl.ds(start, block)], value_buf.at[slot], load_sem.at[1, slot]
            ),
        )

    for copy in load(lo, 0):
        copy.start()
    for which in range(2):
        for j in range(own_pages):
            page_copy(which, j).start()
    top[...] = jnp.full_like(top, -1e30)
    acc[...] = jnp.zeros_like(acc)
    ones = jnp.ones((block, HEAD_DIM), jnp.bfloat16)
    scale = HEAD_DIM ** (-0.5) * LOG2E

    @pl.loop(lo, hi)
    def _(number):
        slot = lax.rem(number - lo, 2)
        for copy in load(number, slot):
            copy.wait()

        @pl.when(number + 1 < hi)
        def _():
            for copy in load(number + 1, 1 - slot):
                copy.start()

        allowed = query_segs[:, 0:1] == key_segs[number]
        for h in range(heads):
            part = pl.ds(h * HEAD_DIM, HEAD_DIM)
            scores = lax.dot_general(
                query[:, part], key_buf[slot, :, part], (((1,), (1,)), ((), ())),
                preferred_element_type=jnp.float32,
            ) * scale
            scores = jnp.where(allowed, scores, -1e30)
            old = top[h]
            new = jnp.maximum(old, jnp.max(scores, axis=1, keepdims=True))
            top[h] = new
            weights = jnp.where(allowed, jnp.exp2(scores - new[:, 0:1]), 0.0)
            factor = jnp.exp2(old - new)
            mixed = jnp.dot(
                weights.astype(jnp.bfloat16),
                jnp.concatenate([value_buf[slot, :, part], ones], axis=1),
                preferred_element_type=jnp.float32,
            )
            acc[h] = acc[h] * jnp.concatenate([factor, factor], axis=1) + mixed

    for h in range(heads):
        part = pl.ds(h * HEAD_DIM, HEAD_DIM)
        attended[:, part] = (acc[h, :, :HEAD_DIM] / acc[h, :, HEAD_DIM:]).astype(attended.dtype)
    for which in range(2):
        for j in range(own_pages):
            page_copy(which, j).wait()


def attend(query, keys, values, segment_ids, page_table):
    rows, width = query.shape
    heads = width // HEAD_DIM
    tokens = keys.shape[0]
    row = lax.axis_index("row")
    query_segs = lax.dynamic_slice_in_dim(segment_ids, row * rows, rows, 0)
    first, last = query_segs[0], query_segs[-1]
    lo = jnp.sum(segment_ids < first) // KEY_BLOCK
    hi = (jnp.sum(segment_ids <= last) + KEY_BLOCK - 1) // KEY_BLOCK
    own_pages = rows // PAGE
    slots = row * own_pages + jnp.arange(own_pages)
    numbers = jnp.arange(page_table.shape[0], dtype=jnp.int32)
    owned = jnp.sum(jnp.where(page_table[None] == slots[:, None], numbers[None], 0), axis=1)
    plan = jnp.concatenate([jnp.stack([lo, hi]).astype(jnp.int32), owned.astype(jnp.int32)])
    any_spec = pl.BlockSpec(memory_space=pl.ANY)
    vmem = pl.BlockSpec(memory_space=pltpu.VMEM)
    return pl.pallas_call(
        attend_kernel,
        out_shape=(
            jax.ShapeDtypeStruct((rows, width), jnp.bfloat16),
            jax.ShapeDtypeStruct((2, own_pages, PAGE, width), jnp.bfloat16),
        ),
        in_specs=[
            pl.BlockSpec(memory_space=pltpu.SMEM), vmem, any_spec, any_spec, vmem, vmem,
        ],
        out_specs=(vmem, any_spec),
        scratch_shapes=[
            pltpu.VMEM((2, KEY_BLOCK, width), jnp.bfloat16),
            pltpu.VMEM((2, KEY_BLOCK, width), jnp.bfloat16),
            pltpu.VMEM((heads, rows, HEAD_DIM), jnp.float32),
            pltpu.VMEM((heads, rows, 2 * HEAD_DIM), jnp.float32),
            pltpu.SemaphoreType.DMA((2, 2)),
            pltpu.SemaphoreType.DMA((2, own_pages)),
        ],
        compiler_params=pltpu.CompilerParams(vmem_limit_bytes=40 * 2**20),
        name="attend",
    )(
        plan, query, keys, values, query_segs[:, None],
        segment_ids.reshape(tokens // KEY_BLOCK, 1, KEY_BLOCK),
    )


def body(
    hidden, modulation, w_query, w_key, w_value, q_gain, k_gain, positions, segment_ids, page_table
):
    query, keys, values = project(
        hidden, modulation, w_query, w_key, w_value, q_gain, k_gain, positions
    )
    tokens, width = segment_ids.shape[0], hidden.shape[1]
    return attend(
        query, keys.reshape(tokens, width), values.reshape(tokens, width), segment_ids, page_table
    )


def solution(mesh):
    in_specs = (
        P("row", "col"),
        P(),
        P("row", "col"),
        P("row", "col"),
        P("row", "col"),
        P("col"),
        P("col"),
        P(None, "row"),
        P(),
        P(),
    )
    out_specs = (P("row", "col"), P(None, "row", None, "col"))
    return jax.shard_map(body, mesh=mesh, in_specs=in_specs, out_specs=out_specs, check_vma=False)
```

```python
import jax
import jax.numpy as jnp
import numpy as np
from jax import lax
from jax.experimental import pallas as pl
from jax.experimental.pallas import tpu as pltpu
from jax.sharding import PartitionSpec as P

HEAD_DIM = 128
PAGE = 128
LOG2E = 1.4426950408889634
epsilon = 1e-06


def rotary_rates(pair_count):
    frame_pairs = pair_count - 2 * (pair_count // 3)
    side_pairs = pair_count // 3
    column = np.arange(pair_count)
    starts = [0, frame_pairs, frame_pairs + side_pairs, pair_count]
    rates = np.zeros((8, 2 * pair_count), np.float32)
    for i in range(3):
        count = starts[i + 1] - starts[i]
        rate = np.power(10000.0, -(column - starts[i]) / count).astype(np.float32)
        inside = (column >= starts[i]) & (column < starts[i + 1])
        rates[i] = np.repeat(np.where(inside, rate, 0.0), 2)
    return rates


class Ring:
    def __init__(self, net, name, own, buffer, pair_first, sibling):
        self.net, self.name, self.own, self.buffer = net, name, own, buffer
        self.pair_first, self.sibling = pair_first, sibling

    def view(self, pair, step, half=None, other=False):
        return self.buffer(self.net.slot(self.name, pair, step, other), half)

    def put(self, source, target, kind, link):
        self.net.put(source, target, (self.name, kind), self.net.device(self.name, link))

    def got(self, kind, view):
        self.net.got(view, (self.name, kind))

    def start(self):
        mine = self.view(0, 0)
        if self.pair_first:
            self.put(self.own, mine, "p", "pair")
        self.put(self.own, mine, "m", "up")
        self.put(self.own, mine, "n", "down")
        if not self.pair_first:
            self.put(self.own, mine, "p", "pair")
        if self.sibling:
            self.put(self.own, mine, "so", "core")
        self.net.local(self.own, mine)

    def share(self, kind, view):
        if self.sibling:
            self.put(view, view, "s" + kind, "core")

    def events(self):
        def pair():
            view = self.view(1, 0)
            self.got("p", view)
            if self.pair_first:
                self.put(view, view, "pm", "up")
                self.put(view, view, "pn", "down")
            self.share("p", view)

        def ring(prefix, where, direction):
            def run():
                step, kind, half, link = (
                    (-1, "m", 0, "up") if direction == 0 else (1, "n", 1, "down")
                )
                view = self.view(where, step)
                self.got(prefix + kind, view)
                if where == 0 or self.pair_first:
                    part = self.view(where, step, half)
                    self.put(part, part, prefix + ("a", "b")[direction], link)
                if where == 0 and not self.pair_first:
                    self.put(view, view, "p" + kind, "pair")
                self.share(prefix + kind, view)

            return run

        def far(prefix, where):
            def run():
                view = self.view(where, 2)
                if where == 0 or self.pair_first:
                    for half, kind in enumerate("ab"):
                        self.got(prefix + kind, self.view(where, 2, half))
                else:
                    self.got(prefix + "f", view)
                if where == 0 and not self.pair_first:
                    self.put(view, view, "pf", "pair")
                self.share(prefix + "f", view)

            return run

        near = [ring("", 0, 0), ring("", 0, 1)]
        crossed = [ring("p", 1, 0), ring("p", 1, 1)]
        if self.pair_first:
            return [pair, *near, *crossed, far("", 0), far("p", 1)]
        return [*near, pair, far("", 0), *crossed, far("p", 1)]

    def met(self, pair, step):
        kind = {0: "p" if pair else "o", -1: "m", 1: "n", 2: "f"}[step]
        prefix = "p" if pair and step else ""
        self.got("s" + prefix + kind, self.view(pair, step, other=True))

    def finish(self):
        for pair in (0, 1):
            for step in (0, -1, 1, 2):
                self.met(pair, step)


class Net:
    def __init__(self, send, recv, own_sem):
        self.send, self.recv, self.own_sem = send, recv, own_sem
        self.sent, self.kinds, self.locals = [], {}, []
        row, col = lax.axis_index("row"), lax.axis_index("col")
        self.row, self.col = row, col
        self.core, self.y, self.z_lo = row % 2, (row // 2) % 4, row // 8
        self.x, self.z_hi = col % 4, col // 4

    def row_at(self, pair, step, other):
        z_lo = 1 - self.z_lo if pair else self.z_lo
        core = 1 - self.core if other else self.core
        return z_lo * 8 + ((self.y + step + 4) % 4) * 2 + core

    def col_at(self, pair, step):
        z_hi = 1 - self.z_hi if pair else self.z_hi
        return z_hi * 4 + (self.x + step + 4) % 4

    def slot(self, name, pair, step, other):
        return self.col_at(pair, step) if name == "x" else self.row_at(pair, step, other)

    def device(self, name, link):
        pair, step = {"pair": (1, 0), "up": (0, 1), "down": (0, -1), "core": (0, 0)}[link]
        if name == "x":
            return (self.row, self.col_at(pair, step))
        return (self.row_at(pair, step, link == "core"), self.col)

    def partners(self):
        rows = [self.device("w", link) for link in ("pair", "up", "down", "core")]
        return rows + self.peers()

    def peers(self):
        others = [(p, s) for p in (0, 1) for s in range(4) if (p, s) != (0, 0)]
        return [(self.row, self.col_at(*o)) for o in others]

    def number(self, kind):
        return self.kinds.setdefault(kind, len(self.kinds))

    def copy(self, source, target, kind, device):
        return pltpu.make_async_remote_copy(
            src_ref=source,
            dst_ref=target,
            send_sem=self.send.at[len(self.sent)],
            recv_sem=self.recv.at[self.number(kind)],
            device_id=device,
            device_id_type=pl.DeviceIdType.MESH,
        )

    def put(self, source, target, kind, device):
        copy = self.copy(source, target, kind, device)
        copy.start()
        self.sent.append(copy)

    def got(self, view, kind):
        pltpu.make_async_remote_copy(
            src_ref=view,
            dst_ref=view,
            send_sem=self.send.at[0],
            recv_sem=self.recv.at[self.number(kind)],
            device_id=self.device("w", "core"),
            device_id_type=pl.DeviceIdType.MESH,
        ).wait_recv()

    def local(self, source, target):
        copy = pltpu.make_async_copy(source, target, self.own_sem.at[len(self.locals)])
        copy.start()
        self.locals.append(copy)


def attention_kernel(
    hidden, modulation, w_query, w_key, w_value, q_gain, k_gain, positions, segs, rates,
    attended, keys_all, values_all,
    hidden_all, modulated, weights, raw, key_own, value_own, squares, tables,
    query_own, marks, key_buf, value_buf, top, acc,
    send, recv, own_sem, load_sem,
):
    net = Net(send, recv, own_sem)
    rows, width = hidden.shape
    deep = w_query.shape[0]
    features = modulation.shape[1]
    heads = width // HEAD_DIM

    barrier = pltpu.get_barrier_semaphore()
    partners = net.partners()
    for device in partners:
        pl.semaphore_signal(
            barrier, inc=1, device_id=device, device_id_type=pl.DeviceIdType.MESH
        )
    pl.semaphore_wait(barrier, len(partners))

    def cut(start, size, half):
        if half is None:
            return pl.ds(pl.multiple_of(start, 16), size)
        return pl.ds(pl.multiple_of(start + half * (size // 2), 16), size // 2)

    def weight_view(which):
        return lambda slot, half: weights.at[which, cut(slot * deep, deep, half)]

    def token_view(ref):
        return lambda slot, half: ref.at[slot, cut(0, rows, half)]

    hid = Ring(net, "x", hidden, token_view(hidden_all), True, False)
    wk = Ring(net, "wk", w_key, weight_view(1), True, True)
    wv = Ring(net, "wv", w_value, weight_view(2), False, True)
    wq = Ring(net, "wq", w_query, weight_view(0), True, True)
    kk = Ring(net, "kk", key_own, token_view(keys_all), True, True)
    vv = Ring(net, "vv", value_own, token_view(values_all), False, True)

    def pull(*queues):
        queues = [list(q) for q in queues]
        while any(queues):
            for q in queues:
                if q:
                    q.pop(0)()

    hid.start()
    wv.start()
    wk.start()

    def column(line):
        return jnp.broadcast_to(line, (HEAD_DIM, line.shape[1])).T

    angle = jnp.zeros((rows, HEAD_DIM), jnp.float32)
    for i in range(3):
        angle = angle + column(positions[i : i + 1, :].astype(jnp.float32)) * rates[i : i + 1]
    lane = lax.broadcasted_iota(jnp.int32, angle.shape, 1)
    even = lane % 2 == 0
    tables[0] = jnp.cos(angle)
    sine = jnp.sin(angle)
    tables[1] = jnp.where(even, -sine, sine)

    @pl.loop(0, segs.shape[0])
    def _(i):
        numbers = column(segs[pl.ds(i, 1), :].astype(jnp.float32))
        lanes = lax.broadcasted_iota(jnp.int32, numbers.shape, 1).astype(jnp.float32)
        part = pl.ds(pl.multiple_of(i * HEAD_DIM, HEAD_DIM), HEAD_DIM)
        marks[part, :] = jnp.where(numbers == lanes, 0.0, -1.0).astype(jnp.bfloat16)

    def normalise():
        net.locals[0].wait()
        groups = hidden_all.shape[0]

        def add(g, total):
            return total + jnp.sum(hidden_all[g].astype(jnp.float32), axis=1, keepdims=True)

        zero = jnp.zeros((rows, 1), jnp.float32)
        average = lax.fori_loop(0, groups, add, zero) / features

        def spread(g, total):
            centred = hidden_all[g].astype(jnp.float32) - average
            return total + jnp.sum(centred * centred, axis=1, keepdims=True)

        variance = lax.fori_loop(0, groups, spread, zero) / features
        scale = lax.rsqrt(variance + epsilon)

        @pl.loop(0, groups)
        def _(g):
            part = pl.ds(pl.multiple_of(g * width, width), width)
            normed = (hidden_all[g].astype(jnp.float32) - average) * scale
            shifted = normed * (1.0 + modulation[1:2, part]) + modulation[0:1, part]
            modulated[:, part] = shifted.astype(jnp.bfloat16)

    def project(which):
        step = 2 * width
        raw[...] = jnp.zeros_like(raw)

        @pl.loop(0, features // step)
        def _(g):
            part = pl.ds(pl.multiple_of(g * step, step), step)
            raw[...] += jnp.dot(
                modulated[:, part], weights[which, part, :], preferred_element_type=jnp.float32
            )

    def send_squares(number):
        whole = raw[...]
        part = jnp.zeros((rows, HEAD_DIM), jnp.float32)
        for h in range(heads):
            piece = whole[:, h * HEAD_DIM : (h + 1) * HEAD_DIM]
            part = part + piece * piece
        total = jnp.sum(part.T, axis=0, keepdims=True)
        mine = squares.at[number, net.col]
        squares[number, net.col] = jnp.broadcast_to(total, (8, rows))
        for i, device in enumerate(net.peers()):
            net.put(mine, mine, ("sq", number, i), device)

    def turned(number, gain, scale):
        others = [(p, s) for p in (0, 1) for s in range(4) if (p, s) != (0, 0)]
        for i, (pair, step) in enumerate(others):
            net.got(squares.at[number, net.col_at(pair, -step)], ("sq", number, i))
        total = jnp.sum(squares[number], axis=0)
        factor = lax.rsqrt(column(total[0:1]) / features + epsilon) * scale
        made = []
        for h in range(heads):
            normed = raw[:, h * HEAD_DIM : (h + 1) * HEAD_DIM] * factor * gain[h : h + 1, :]
            swapped = jnp.where(
                even, pltpu.roll(normed, HEAD_DIM - 1, 1), pltpu.roll(normed, 1, 1)
            )
            made.append((normed * tables[0] + swapped * tables[1]).astype(jnp.bfloat16))
        return made

    def loads(chip, slot):
        for i, (source, target) in enumerate(((keys_all, key_buf), (values_all, value_buf))):
            for core in range(2):
                yield pltpu.make_async_copy(
                    source.at[chip * 2 + core],
                    target.at[slot, pl.ds(core * rows, rows)],
                    load_sem.at[slot, 2 * i + core],
                )

    ones = jnp.ones((2 * rows, HEAD_DIM), jnp.bfloat16)

    def attend(chip, slot):
        for copy in loads(chip, slot):
            copy.wait()
        key_marks = marks[pl.ds(pl.multiple_of(chip * 2 * rows, HEAD_DIM), 2 * rows), :]
        for h in range(heads):
            part = slice(h * HEAD_DIM, (h + 1) * HEAD_DIM)
            scores = lax.dot_general(
                query_own[h],
                jnp.concatenate([key_buf[slot, :, part], key_marks], axis=1),
                (((1,), (1,)), ((), ())),
                preferred_element_type=jnp.float32,
            )
            old = top[h]
            new = jnp.maximum(old, jnp.max(scores, axis=1, keepdims=True))
            top[h] = new
            chances = jnp.exp2(scores - new[:, 0:1])
            factor = jnp.exp2(old - new)
            mixed = jnp.dot(
                chances.astype(jnp.bfloat16),
                jnp.concatenate([value_buf[slot, :, part], ones], axis=1),
                preferred_element_type=jnp.float32,
            )
            acc[h] = acc[h] * jnp.concatenate([factor, factor], axis=1) + mixed

    waiting = []

    def block(pair, step):
        chip = net.row_at(pair, step, False) // 2
        if (pair, step) == (0, 0):
            for copy in net.locals[4:6]:
                copy.wait()
        for ring in (kk, vv):
            ring.met(pair, step)
        slot = block_count[0] % 2
        block_count[0] += 1
        for copy in loads(chip, slot):
            copy.start()
        if waiting:
            attend(*waiting.pop())
        waiting.append((chip, slot))

    block_count = [0]

    v_steps, k_steps, q_steps = wv.events(), wk.events(), wq.events()
    x_steps = hid.events()
    pull(v_steps[:5], k_steps[:5], x_steps[:5])
    wq.start()
    pull(v_steps[5:6], k_steps[5:6], x_steps[5:7])
    normalise()
    pull(v_steps[6:7], k_steps[6:7])
    wv.finish()
    for copy in net.locals[1:3]:
        copy.wait()
    project(2)
    value_own[...] = raw[...].astype(jnp.bfloat16)
    vv.start()
    wk.finish()
    project(1)
    send_squares(0)
    pull(q_steps[:3])
    key_own[...] = jnp.concatenate(turned(0, k_gain, 1.0), axis=1)
    kk.start()
    v_steps, k_steps = vv.events(), kk.events()
    pull(q_steps[3:], v_steps[:3], k_steps[:3])
    wq.finish()
    net.locals[3].wait()
    project(0)
    send_squares(1)
    top[...] = jnp.full_like(top, -1e20)
    acc[...] = jnp.zeros_like(acc)
    pull(v_steps[3:4], k_steps[3:5])
    own_start = pl.multiple_of(net.row * rows, HEAD_DIM)
    own_marks = marks[pl.ds(own_start, rows), :].astype(jnp.float32)
    query_marks = ((own_marks + 1.0) * 1e30).astype(jnp.bfloat16)
    for h, piece in enumerate(turned(1, q_gain, HEAD_DIM ** (-0.5) * LOG2E)):
        query_own[h] = jnp.concatenate([piece, query_marks], axis=1)
    block(0, 0)
    block(0, -1)
    block(0, 1)
    pull(v_steps[4:6], k_steps[5:6])
    block(1, 0)
    block(1, -1)
    block(1, 1)
    pull(v_steps[6:7], k_steps[6:7])
    block(0, 2)
    block(1, 2)
    attend(*waiting.pop())
    for h in range(heads):
        part = slice(h * HEAD_DIM, (h + 1) * HEAD_DIM)
        attended[:, part] = (acc[h, :, :HEAD_DIM] / acc[h, :, HEAD_DIM:]).astype(attended.dtype)
    for copy in net.sent:
        copy.wait_send()


def pages_kernel(page_table, result, keys, values, attended, pages, sem):
    own_pages = pages.shape[1]
    first = lax.axis_index("row") * own_pages

    def look(b, found):
        return tuple(
            jnp.where(page_table[b] == first + j, b, found[j]) for j in range(own_pages)
        )

    start = tuple(jnp.int32(0) for _ in range(own_pages))
    found = lax.fori_loop(0, page_table.shape[0], look, start)
    copies = [pltpu.make_async_copy(result, attended, sem.at[2 * own_pages])]
    for i, source in enumerate((keys, values)):
        for j in range(own_pages):
            rows = pl.ds(pl.multiple_of(found[j] * PAGE, PAGE), PAGE)
            copies.append(
                pltpu.make_async_copy(source.at[rows], pages.at[i, j], sem.at[i * own_pages + j])
            )
    for copy in copies:
        copy.start()
    for copy in copies:
        copy.wait()


def store_pages(page_table, result, keys, values):
    rows, width = result.shape
    any_spec = pl.BlockSpec(memory_space=pl.ANY)
    own_pages = rows // PAGE
    return pl.pallas_call(
        pages_kernel,
        out_shape=(
            jax.ShapeDtypeStruct((rows, width), jnp.bfloat16),
            jax.ShapeDtypeStruct((2, own_pages, PAGE, width), jnp.bfloat16),
        ),
        in_specs=[pl.BlockSpec(memory_space=pltpu.SMEM), any_spec, any_spec, any_spec],
        out_specs=(any_spec, any_spec),
        scratch_shapes=[pltpu.SemaphoreType.DMA((2 * own_pages + 1,))],
        compiler_params=pltpu.CompilerParams(vmem_limit_bytes=60 * 2**20),
        name="pages",
    )(page_table, result, keys, values)


def body(
    hidden, modulation, w_query, w_key, w_value, q_gain, k_gain, positions, segment_ids, page_table
):
    rows, width = hidden.shape
    deep = w_query.shape[0]
    features = modulation.shape[1]
    tokens = segment_ids.shape[0]
    members, groups, heads = features // deep, features // width, width // HEAD_DIM
    any_spec = pl.BlockSpec(memory_space=pl.ANY)
    vmem = pl.BlockSpec(memory_space=pltpu.VMEM)
    shards = jax.ShapeDtypeStruct((members, rows, width), jnp.bfloat16)
    attended, keys, values = pl.pallas_call(
        attention_kernel,
        out_shape=(jax.ShapeDtypeStruct((rows, width), jnp.bfloat16), shards, shards),
        in_specs=[any_spec, vmem, any_spec, any_spec, any_spec, vmem, vmem, vmem, vmem, vmem],
        out_specs=(vmem, any_spec, any_spec),
        scratch_shapes=[
            pltpu.VMEM((groups, rows, width), jnp.bfloat16),
            pltpu.VMEM((rows, features), jnp.bfloat16),
            pltpu.VMEM((3, features, width), jnp.bfloat16),
            pltpu.VMEM((rows, width), jnp.float32),
            pltpu.VMEM((rows, width), jnp.bfloat16),
            pltpu.VMEM((rows, width), jnp.bfloat16),
            pltpu.VMEM((2, groups, 8, rows), jnp.float32),
            pltpu.VMEM((2, rows, HEAD_DIM), jnp.float32),
            pltpu.VMEM((heads, rows, 2 * HEAD_DIM), jnp.bfloat16),
            pltpu.VMEM((tokens, HEAD_DIM), jnp.bfloat16),
            pltpu.VMEM((2, 2 * rows, width), jnp.bfloat16),
            pltpu.VMEM((2, 2 * rows, width), jnp.bfloat16),
            pltpu.VMEM((heads, rows, HEAD_DIM), jnp.float32),
            pltpu.VMEM((heads, rows, 2 * HEAD_DIM), jnp.float32),
            pltpu.SemaphoreType.DMA((128,)),
            pltpu.SemaphoreType.DMA((128,)),
            pltpu.SemaphoreType.DMA((6,)),
            pltpu.SemaphoreType.DMA((2, 4)),
        ],
        compiler_params=pltpu.CompilerParams(
            collective_id=0, has_side_effects=True, vmem_limit_bytes=58 * 2**20
        ),
        name="attention",
    )(
        hidden, modulation, w_query, w_key, w_value,
        q_gain.reshape(heads, HEAD_DIM), k_gain.reshape(heads, HEAD_DIM), positions,
        segment_ids.reshape(tokens // HEAD_DIM, HEAD_DIM),
        jnp.asarray(rotary_rates(HEAD_DIM // 2)),
    )
    return store_pages(
        page_table, attended, keys.reshape(tokens, width), values.reshape(tokens, width)
    )


def solution(mesh):
    in_specs = (
        P("row", "col"),
        P(),
        P("row", "col"),
        P("row", "col"),
        P("row", "col"),
        P("col"),
        P("col"),
        P(None, "row"),
        P(),
        P(),
    )
    out_specs = (P("row", "col"), P(None, "row", None, "col"))
    return jax.shard_map(body, mesh=mesh, in_specs=in_specs, out_specs=out_specs, check_vma=False)
```

```python
import jax
import jax.numpy as jnp
import numpy as np
from jax import lax
from jax.experimental import pallas as pl
from jax.experimental.pallas import tpu as pltpu
from jax.sharding import PartitionSpec as P

HEAD_DIM = 128
PAGE = 128
LOG2E = 1.4426950408889634
epsilon = 1e-06


def rotary_rates(pair_count):
    frame_pairs = pair_count - 2 * (pair_count // 3)
    side_pairs = pair_count // 3
    column = np.arange(pair_count)
    starts = [0, frame_pairs, frame_pairs + side_pairs, pair_count]
    rates = np.zeros((8, 2 * pair_count), np.float32)
    for i in range(3):
        count = starts[i + 1] - starts[i]
        rate = np.power(10000.0, -(column - starts[i]) / count).astype(np.float32)
        inside = (column >= starts[i]) & (column < starts[i + 1])
        rates[i] = np.repeat(np.where(inside, rate, 0.0), 2)
    return rates


class Ring:
    def __init__(self, net, name, own, buffer, pair_first, sibling):
        self.net, self.name, self.own, self.buffer = net, name, own, buffer
        self.pair_first, self.sibling = pair_first, sibling

    def view(self, pair, step, half=None, other=False):
        return self.buffer(self.net.slot(self.name, pair, step, other), half)

    def put(self, source, target, kind, link):
        self.net.put(source, target, (self.name, kind), self.net.device(self.name, link))

    def got(self, kind, view):
        self.net.got(view, (self.name, kind))

    def start(self):
        mine = self.view(0, 0)
        if self.pair_first:
            self.put(self.own, mine, "p", "pair")
        self.put(self.own, mine, "m", "up")
        self.put(self.own, mine, "n", "down")
        if not self.pair_first:
            self.put(self.own, mine, "p", "pair")
        if self.sibling:
            self.put(self.own, mine, "so", "core")
        self.net.local(self.own, mine)

    def share(self, kind, view):
        if self.sibling:
            self.put(view, view, "s" + kind, "core")

    def events(self):
        def pair():
            view = self.view(1, 0)
            self.got("p", view)
            if self.pair_first:
                self.put(view, view, "pm", "up")
                self.put(view, view, "pn", "down")
            self.share("p", view)

        def ring(prefix, where, direction):
            def run():
                step, kind, half, link = (
                    (-1, "m", 0, "up") if direction == 0 else (1, "n", 1, "down")
                )
                view = self.view(where, step)
                self.got(prefix + kind, view)
                if where == 0 or self.pair_first:
                    part = self.view(where, step, half)
                    self.put(part, part, prefix + ("a", "b")[direction], link)
                if where == 0 and not self.pair_first:
                    self.put(view, view, "p" + kind, "pair")
                self.share(prefix + kind, view)

            return run

        def far(prefix, where):
            def run():
                view = self.view(where, 2)
                if where == 0 or self.pair_first:
                    for half, kind in enumerate("ab"):
                        self.got(prefix + kind, self.view(where, 2, half))
                else:
                    self.got(prefix + "f", view)
                if where == 0 and not self.pair_first:
                    self.put(view, view, "pf", "pair")
                self.share(prefix + "f", view)

            return run

        near = [ring("", 0, 0), ring("", 0, 1)]
        crossed = [ring("p", 1, 0), ring("p", 1, 1)]
        if self.pair_first:
            return [pair, *near, *crossed, far("", 0), far("p", 1)]
        return [*near, pair, far("", 0), *crossed, far("p", 1)]

    def met(self, pair, step):
        kind = {0: "p" if pair else "o", -1: "m", 1: "n", 2: "f"}[step]
        prefix = "p" if pair and step else ""
        self.got("s" + prefix + kind, self.view(pair, step, other=True))

    def finish(self):
        for pair in (0, 1):
            for step in (0, -1, 1, 2):
                self.met(pair, step)


class Net:
    def __init__(self, send, recv, own_sem):
        self.send, self.recv, self.own_sem = send, recv, own_sem
        self.sent, self.kinds, self.locals = [], {}, []
        row, col = lax.axis_index("row"), lax.axis_index("col")
        self.row, self.col = row, col
        self.core, self.y, self.z_lo = row % 2, (row // 2) % 4, row // 8
        self.x, self.z_hi = col % 4, col // 4

    def row_at(self, pair, step, other):
        z_lo = 1 - self.z_lo if pair else self.z_lo
        core = 1 - self.core if other else self.core
        return z_lo * 8 + ((self.y + step + 4) % 4) * 2 + core

    def col_at(self, pair, step):
        z_hi = 1 - self.z_hi if pair else self.z_hi
        return z_hi * 4 + (self.x + step + 4) % 4

    def slot(self, name, pair, step, other):
        return self.col_at(pair, step) if name == "x" else self.row_at(pair, step, other)

    def device(self, name, link):
        pair, step = {"pair": (1, 0), "up": (0, 1), "down": (0, -1), "core": (0, 0)}[link]
        if name == "x":
            return (self.row, self.col_at(pair, step))
        return (self.row_at(pair, step, link == "core"), self.col)

    def partners(self):
        rows = [self.device("w", link) for link in ("pair", "up", "down", "core")]
        return rows + self.peers()

    def peers(self):
        others = [(p, s) for p in (0, 1) for s in range(4) if (p, s) != (0, 0)]
        return [(self.row, self.col_at(*o)) for o in others]

    def number(self, kind):
        return self.kinds.setdefault(kind, len(self.kinds))

    def copy(self, source, target, kind, device):
        return pltpu.make_async_remote_copy(
            src_ref=source,
            dst_ref=target,
            send_sem=self.send.at[len(self.sent)],
            recv_sem=self.recv.at[self.number(kind)],
            device_id=device,
            device_id_type=pl.DeviceIdType.MESH,
        )

    def put(self, source, target, kind, device):
        copy = self.copy(source, target, kind, device)
        copy.start()
        self.sent.append(copy)

    def got(self, view, kind):
        pltpu.make_async_remote_copy(
            src_ref=view,
            dst_ref=view,
            send_sem=self.send.at[0],
            recv_sem=self.recv.at[self.number(kind)],
            device_id=self.device("w", "core"),
            device_id_type=pl.DeviceIdType.MESH,
        ).wait_recv()

    def local(self, source, target):
        copy = pltpu.make_async_copy(source, target, self.own_sem.at[len(self.locals)])
        copy.start()
        self.locals.append(copy)


def attention_kernel(
    hidden, modulation, w_query, w_key, w_value, q_gain, k_gain, positions, segs, rates,
    attended, keys_all, values_all,
    hidden_all, modulated, weights, raw, key_own, value_own, squares, tables,
    query_own, marks, key_buf, value_buf, top, acc,
    send, recv, own_sem, load_sem,
):
    net = Net(send, recv, own_sem)
    rows, width = hidden.shape
    deep = w_query.shape[0]
    features = modulation.shape[1]
    heads = width // HEAD_DIM

    barrier = pltpu.get_barrier_semaphore()
    partners = net.partners()
    for device in partners:
        pl.semaphore_signal(
            barrier, inc=1, device_id=device, device_id_type=pl.DeviceIdType.MESH
        )
    pl.semaphore_wait(barrier, len(partners))

    def cut(start, size, half):
        if half is None:
            return pl.ds(pl.multiple_of(start, 16), size)
        return pl.ds(pl.multiple_of(start + half * (size // 2), 16), size // 2)

    def weight_view(which):
        return lambda slot, half: weights.at[which, cut(slot * deep, deep, half)]

    def token_view(ref):
        return lambda slot, half: ref.at[slot, cut(0, ref.shape[1], half)]

    hid = Ring(net, "x", hidden, token_view(hidden_all), True, False)
    wk = Ring(net, "wk", w_key, weight_view(1), True, True)
    wv = Ring(net, "wv", w_value, weight_view(2), False, True)
    wq = Ring(net, "wq", w_query, weight_view(0), True, True)
    kk = Ring(net, "kk", key_own, token_view(keys_all), True, True)
    vv = Ring(net, "vv", value_own, token_view(values_all), False, True)

    def pull(*queues):
        queues = [list(q) for q in queues]
        while any(queues):
            for q in queues:
                if q:
                    q.pop(0)()

    hid.start()
    wv.start()
    wk.start()

    def column(line):
        return jnp.broadcast_to(line, (HEAD_DIM, line.shape[1])).T

    angle = jnp.zeros((rows, HEAD_DIM), jnp.float32)
    for i in range(3):
        angle = angle + column(positions[i : i + 1, :].astype(jnp.float32)) * rates[i : i + 1]
    lane = lax.broadcasted_iota(jnp.int32, angle.shape, 1)
    even = lane % 2 == 0
    tables[0] = jnp.cos(angle)
    sine = jnp.sin(angle)
    tables[1] = jnp.where(even, -sine, sine)

    @pl.loop(0, segs.shape[0])
    def _(i):
        numbers = jnp.broadcast_to(segs[pl.ds(i, 1), :], (HEAD_DIM, HEAD_DIM))
        kinds = lax.broadcasted_iota(jnp.int32, numbers.shape, 0)
        part = pl.ds(pl.multiple_of(i * HEAD_DIM, HEAD_DIM), HEAD_DIM)
        marks[:, part] = jnp.where(numbers == kinds, 0.0, -1.0).astype(jnp.bfloat16)

    def normalise():
        net.locals[0].wait()
        groups = hidden_all.shape[0]

        def add(g, total):
            return total + jnp.sum(hidden_all[g].astype(jnp.float32), axis=1, keepdims=True)

        zero = jnp.zeros((rows, 1), jnp.float32)
        average = lax.fori_loop(0, groups, add, zero) / features

        def spread(g, total):
            centred = hidden_all[g].astype(jnp.float32) - average
            return total + jnp.sum(centred * centred, axis=1, keepdims=True)

        variance = lax.fori_loop(0, groups, spread, zero) / features
        scale = lax.rsqrt(variance + epsilon)

        @pl.loop(0, groups)
        def _(g):
            part = pl.ds(pl.multiple_of(g * width, width), width)
            normed = (hidden_all[g].astype(jnp.float32) - average) * scale
            shifted = normed * (1.0 + modulation[1:2, part]) + modulation[0:1, part]
            modulated[:, part] = shifted.astype(jnp.bfloat16)

    def project(which):
        step = 2 * width
        raw[...] = jnp.zeros_like(raw)

        @pl.loop(0, features // step)
        def _(g):
            part = pl.ds(pl.multiple_of(g * step, step), step)
            raw[...] += jnp.dot(
                modulated[:, part], weights[which, part, :], preferred_element_type=jnp.float32
            )

    def send_squares(number):
        whole = raw[...]
        part = jnp.zeros((rows, HEAD_DIM), jnp.float32)
        for h in range(heads):
            piece = whole[:, h * HEAD_DIM : (h + 1) * HEAD_DIM]
            part = part + piece * piece
        total = jnp.sum(part.T, axis=0, keepdims=True)
        mine = squares.at[number, net.col]
        squares[number, net.col] = jnp.broadcast_to(total, (8, rows))
        for i, device in enumerate(net.peers()):
            net.put(mine, mine, ("sq", number, i), device)

    def turned(number, gain, scale):
        others = [(p, s) for p in (0, 1) for s in range(4) if (p, s) != (0, 0)]
        for i, (pair, step) in enumerate(others):
            net.got(squares.at[number, net.col_at(pair, -step)], ("sq", number, i))
        total = jnp.sum(squares[number], axis=0)
        factor = lax.rsqrt(column(total[0:1]) / features + epsilon) * scale
        made = []
        for h in range(heads):
            normed = raw[:, h * HEAD_DIM : (h + 1) * HEAD_DIM] * factor * gain[h : h + 1, :]
            swapped = jnp.where(
                even, pltpu.roll(normed, HEAD_DIM - 1, 1), pltpu.roll(normed, 1, 1)
            )
            made.append(normed * tables[0] + swapped * tables[1])
        return made

    def loads(chip, slot):
        for i, (source, target) in enumerate(((keys_all, key_buf), (values_all, value_buf))):
            for core in range(2):
                yield pltpu.make_async_copy(
                    source.at[chip * 2 + core],
                    target.at[slot, core],
                    load_sem.at[slot, 2 * i + core],
                )

    ones = jnp.ones((2 * rows, HEAD_DIM), jnp.bfloat16)

    def attend(chip, slot):
        for copy in loads(chip, slot):
            copy.wait()
        chip_start = pl.multiple_of(chip * 2 * rows, HEAD_DIM)
        key_marks = marks[:, pl.ds(chip_start, 2 * rows)]
        for h in range(heads):
            part = slice(h * HEAD_DIM, (h + 1) * HEAD_DIM)
            keys = jnp.concatenate([key_buf[slot, 0, part], key_buf[slot, 1, part]], axis=1)
            scores = jnp.dot(
                query_own[h],
                jnp.concatenate([keys, key_marks], axis=0),
                preferred_element_type=jnp.float32,
            )
            old = top[h]
            new = jnp.maximum(old, jnp.max(scores, axis=1, keepdims=True))
            top[h] = new
            chances = jnp.exp2(scores - new[:, 0:1])
            factor = jnp.exp2(old - new)
            mixed = jnp.dot(
                chances.astype(jnp.bfloat16),
                jnp.concatenate(
                    [value_buf[slot, :, :, part].reshape(2 * rows, HEAD_DIM), ones], axis=1
                ),
                preferred_element_type=jnp.float32,
            )
            acc[h] = acc[h] * jnp.concatenate([factor, factor], axis=1) + mixed

    waiting = []

    def block(pair, step):
        chip = net.row_at(pair, step, False) // 2
        if (pair, step) == (0, 0):
            for copy in net.locals[4:6]:
                copy.wait()
        for ring in (kk, vv):
            ring.met(pair, step)
        slot = block_count[0] % 2
        block_count[0] += 1
        for copy in loads(chip, slot):
            copy.start()
        if waiting:
            attend(*waiting.pop())
        waiting.append((chip, slot))

    block_count = [0]

    v_steps, k_steps, q_steps = wv.events(), wk.events(), wq.events()
    x_steps = hid.events()
    pull(v_steps[:5], k_steps[:5], x_steps[:5])
    wq.start()
    pull(v_steps[5:6], k_steps[5:6], x_steps[5:7])
    normalise()
    pull(v_steps[6:7], k_steps[6:7])
    wv.finish()
    for copy in net.locals[1:3]:
        copy.wait()
    project(2)
    value_own[...] = raw[...].astype(jnp.bfloat16)
    vv.start()
    wk.finish()
    project(1)
    send_squares(0)
    pull(q_steps[:3])
    for h, piece in enumerate(turned(0, k_gain, 1.0)):
        key_own[h * HEAD_DIM : (h + 1) * HEAD_DIM, :] = piece.T.astype(jnp.bfloat16)
    kk.start()
    v_steps, k_steps = vv.events(), kk.events()
    pull(q_steps[3:], v_steps[:3], k_steps[:3])
    wq.finish()
    net.locals[3].wait()
    project(0)
    send_squares(1)
    top[...] = jnp.full_like(top, -1e20)
    acc[...] = jnp.zeros_like(acc)
    pull(v_steps[3:4], k_steps[3:5])
    own_lines = rows // HEAD_DIM
    numbers = jnp.concatenate(
        [
            column(segs[pl.ds(net.row * own_lines + i, 1), :].astype(jnp.float32))
            for i in range(own_lines)
        ],
        axis=0,
    )
    query_marks = jnp.where(numbers == lane.astype(jnp.float32), 1e30, 0.0).astype(jnp.bfloat16)
    for h, piece in enumerate(turned(1, q_gain, HEAD_DIM ** (-0.5) * LOG2E)):
        query_own[h] = jnp.concatenate([piece.astype(jnp.bfloat16), query_marks], axis=1)
    block(0, 0)
    block(0, -1)
    block(0, 1)
    pull(v_steps[4:6], k_steps[5:6])
    block(1, 0)
    block(1, -1)
    block(1, 1)
    block(0, 2)
    attend(*waiting.pop())
    pull(v_steps[6:7], k_steps[6:7])
    block(1, 2)
    attend(*waiting.pop())
    for h in range(heads):
        part = slice(h * HEAD_DIM, (h + 1) * HEAD_DIM)
        attended[:, part] = (acc[h, :, :HEAD_DIM] / acc[h, :, HEAD_DIM:]).astype(attended.dtype)
    for copy in net.sent:
        copy.wait_send()


def pages_kernel(page_table, result, keys, values, attended, pages, turned, sem):
    own_pages = pages.shape[1]
    blocks = keys.shape[2] // PAGE
    first = lax.axis_index("row") * own_pages

    def look(b, found):
        return tuple(
            jnp.where(page_table[b] == first + j, b, found[j]) for j in range(own_pages)
        )

    start = tuple(jnp.int32(0) for _ in range(own_pages))
    found = lax.fori_loop(0, page_table.shape[0], look, start)
    copies = []
    for j in range(own_pages):
        shard = found[j] // blocks
        part = pl.ds(pl.multiple_of((found[j] - shard * blocks) * PAGE, PAGE), PAGE)
        copies.append(
            pltpu.make_async_copy(keys.at[shard, :, part], turned.at[j], sem.at[j])
        )
        copies.append(
            pltpu.make_async_copy(
                values.at[shard, part], pages.at[1, j], sem.at[own_pages + j]
            )
        )
    for copy in copies:
        copy.start()
    attended[...] = result[...]
    for copy in copies:
        copy.wait()
    for j in range(own_pages):
        pages[0, j] = turned[j].T


def store_pages(page_table, result, keys, values):
    rows, width = result.shape
    any_spec = pl.BlockSpec(memory_space=pl.ANY)
    vmem = pl.BlockSpec(memory_space=pltpu.VMEM)
    own_pages = rows // PAGE
    return pl.pallas_call(
        pages_kernel,
        out_shape=(
            jax.ShapeDtypeStruct((rows, width), jnp.bfloat16),
            jax.ShapeDtypeStruct((2, own_pages, PAGE, width), jnp.bfloat16),
        ),
        in_specs=[pl.BlockSpec(memory_space=pltpu.SMEM), vmem, any_spec, any_spec],
        out_specs=(vmem, vmem),
        scratch_shapes=[
            pltpu.VMEM((own_pages, width, PAGE), jnp.bfloat16),
            pltpu.SemaphoreType.DMA((2 * own_pages,)),
        ],
        compiler_params=pltpu.CompilerParams(vmem_limit_bytes=60 * 2**20),
        name="pages",
    )(page_table, result, keys, values)


def body(
    hidden, modulation, w_query, w_key, w_value, q_gain, k_gain, positions, segment_ids, page_table
):
    rows, width = hidden.shape
    deep = w_query.shape[0]
    features = modulation.shape[1]
    tokens = segment_ids.shape[0]
    members, groups, heads = features // deep, features // width, width // HEAD_DIM
    any_spec = pl.BlockSpec(memory_space=pl.ANY)
    vmem = pl.BlockSpec(memory_space=pltpu.VMEM)
    key_shards = jax.ShapeDtypeStruct((members, width, rows), jnp.bfloat16)
    value_shards = jax.ShapeDtypeStruct((members, rows, width), jnp.bfloat16)
    attended, keys, values = pl.pallas_call(
        attention_kernel,
        out_shape=(
            jax.ShapeDtypeStruct((rows, width), jnp.bfloat16), key_shards, value_shards
        ),
        in_specs=[any_spec, vmem, any_spec, any_spec, any_spec, vmem, vmem, vmem, vmem, vmem],
        out_specs=(vmem, any_spec, any_spec),
        scratch_shapes=[
            pltpu.VMEM((groups, rows, width), jnp.bfloat16),
            pltpu.VMEM((rows, features), jnp.bfloat16),
            pltpu.VMEM((3, features, width), jnp.bfloat16),
            pltpu.VMEM((rows, width), jnp.float32),
            pltpu.VMEM((width, rows), jnp.bfloat16),
            pltpu.VMEM((rows, width), jnp.bfloat16),
            pltpu.VMEM((2, groups, 8, rows), jnp.float32),
            pltpu.VMEM((2, rows, HEAD_DIM), jnp.float32),
            pltpu.VMEM((heads, rows, 2 * HEAD_DIM), jnp.bfloat16),
            pltpu.VMEM((HEAD_DIM, tokens), jnp.bfloat16),
            pltpu.VMEM((2, 2, width, rows), jnp.bfloat16),
            pltpu.VMEM((2, 2, rows, width), jnp.bfloat16),
            pltpu.VMEM((heads, rows, HEAD_DIM), jnp.float32),
            pltpu.VMEM((heads, rows, 2 * HEAD_DIM), jnp.float32),
            pltpu.SemaphoreType.DMA((128,)),
            pltpu.SemaphoreType.DMA((128,)),
            pltpu.SemaphoreType.DMA((6,)),
            pltpu.SemaphoreType.DMA((2, 4)),
        ],
        compiler_params=pltpu.CompilerParams(
            collective_id=0, has_side_effects=True, vmem_limit_bytes=58 * 2**20
        ),
        name="attention",
    )(
        hidden, modulation, w_query, w_key, w_value,
        q_gain.reshape(heads, HEAD_DIM), k_gain.reshape(heads, HEAD_DIM), positions,
        segment_ids.reshape(tokens // HEAD_DIM, HEAD_DIM),
        jnp.asarray(rotary_rates(HEAD_DIM // 2)),
    )
    return store_pages(page_table, attended, keys, values)


def solution(mesh):
    in_specs = (
        P("row", "col"),
        P(),
        P("row", "col"),
        P("row", "col"),
        P("row", "col"),
        P("col"),
        P("col"),
        P(None, "row"),
        P(),
        P(),
    )
    out_specs = (P("row", "col"), P(None, "row", None, "col"))
    return jax.shard_map(body, mesh=mesh, in_specs=in_specs, out_specs=out_specs, check_vma=False)
```

```python
import jax
import jax.numpy as jnp
import numpy as np
from jax import lax
from jax.experimental import pallas as pl
from jax.experimental.pallas import tpu as pltpu
from jax.sharding import PartitionSpec as P

HEAD_DIM = 128
PAGE = 128
LOG2E = 1.4426950408889634
epsilon = 1e-06


def rotary_rates(pair_count):
    frame_pairs = pair_count - 2 * (pair_count // 3)
    side_pairs = pair_count // 3
    column = np.arange(pair_count)
    starts = [0, frame_pairs, frame_pairs + side_pairs, pair_count]
    rates = np.zeros((8, 2 * pair_count), np.float32)
    for i in range(3):
        count = starts[i + 1] - starts[i]
        rate = np.power(10000.0, -(column - starts[i]) / count).astype(np.float32)
        inside = (column >= starts[i]) & (column < starts[i + 1])
        rates[i] = np.repeat(np.where(inside, rate, 0.0), 2)
    return rates


class Ring:
    def __init__(self, net, name, own, buffer, pair_first, sibling):
        self.net, self.name, self.own, self.buffer = net, name, own, buffer
        self.pair_first, self.sibling = pair_first, sibling

    def view(self, pair, step, half=None, other=False):
        return self.buffer(self.net.slot(self.name, pair, step, other), half)

    def put(self, source, target, kind, link):
        self.net.put(source, target, (self.name, kind), self.net.device(self.name, link))

    def got(self, kind, view):
        self.net.got(view, (self.name, kind))

    def start(self):
        mine = self.view(0, 0)
        if self.pair_first:
            self.put(self.own, mine, "p", "pair")
        self.put(self.own, mine, "m", "up")
        self.put(self.own, mine, "n", "down")
        if not self.pair_first:
            self.put(self.own, mine, "p", "pair")
        if self.sibling:
            self.put(self.own, mine, "so", "core")
        self.net.local(self.own, mine)

    def share(self, kind, view):
        if self.sibling:
            self.put(view, view, "s" + kind, "core")

    def events(self):
        def pair():
            view = self.view(1, 0)
            self.got("p", view)
            if self.pair_first:
                self.put(view, view, "pm", "up")
                self.put(view, view, "pn", "down")
            self.share("p", view)

        def ring(prefix, where, direction):
            def run():
                step, kind, half, link = (
                    (-1, "m", 0, "up") if direction == 0 else (1, "n", 1, "down")
                )
                view = self.view(where, step)
                self.got(prefix + kind, view)
                if where == 0 or self.pair_first:
                    part = self.view(where, step, half)
                    self.put(part, part, prefix + ("a", "b")[direction], link)
                if where == 0 and not self.pair_first:
                    self.put(view, view, "p" + kind, "pair")
                self.share(prefix + kind, view)

            return run

        def far(prefix, where):
            def run():
                view = self.view(where, 2)
                if where == 0 or self.pair_first:
                    for half, kind in enumerate("ab"):
                        self.got(prefix + kind, self.view(where, 2, half))
                else:
                    self.got(prefix + "f", view)
                if where == 0 and not self.pair_first:
                    self.put(view, view, "pf", "pair")
                self.share(prefix + "f", view)

            return run

        near = [ring("", 0, 0), ring("", 0, 1)]
        crossed = [ring("p", 1, 0), ring("p", 1, 1)]
        if self.pair_first:
            return [pair, *near, *crossed, far("", 0), far("p", 1)]
        return [*near, pair, far("", 0), *crossed, far("p", 1)]

    def met(self, pair, step):
        kind = {0: "p" if pair else "o", -1: "m", 1: "n", 2: "f"}[step]
        prefix = "p" if pair and step else ""
        self.got("s" + prefix + kind, self.view(pair, step, other=True))

    def finish(self):
        for pair in (0, 1):
            for step in (0, -1, 1, 2):
                self.met(pair, step)


class Net:
    def __init__(self, send, recv, own_sem):
        self.send, self.recv, self.own_sem = send, recv, own_sem
        self.sent, self.kinds, self.locals = [], {}, []
        row, col = lax.axis_index("row"), lax.axis_index("col")
        self.row, self.col = row, col
        self.core, self.y, self.z_lo = row % 2, (row // 2) % 4, row // 8
        self.x, self.z_hi = col % 4, col // 4

    def row_at(self, pair, step, other):
        z_lo = 1 - self.z_lo if pair else self.z_lo
        core = 1 - self.core if other else self.core
        return z_lo * 8 + ((self.y + step + 4) % 4) * 2 + core

    def col_at(self, pair, step):
        z_hi = 1 - self.z_hi if pair else self.z_hi
        return z_hi * 4 + (self.x + step + 4) % 4

    def slot(self, name, pair, step, other):
        return self.col_at(pair, step) if name == "x" else self.row_at(pair, step, other)

    def device(self, name, link):
        pair, step = {"pair": (1, 0), "up": (0, 1), "down": (0, -1), "core": (0, 0)}[link]
        if name == "x":
            return (self.row, self.col_at(pair, step))
        return (self.row_at(pair, step, link == "core"), self.col)

    def partners(self):
        rows = [self.device("w", link) for link in ("pair", "up", "down", "core")]
        return rows + self.peers()

    def peers(self):
        others = [(p, s) for p in (0, 1) for s in range(4) if (p, s) != (0, 0)]
        return [(self.row, self.col_at(*o)) for o in others]

    def number(self, kind):
        return self.kinds.setdefault(kind, len(self.kinds))

    def copy(self, source, target, kind, device):
        return pltpu.make_async_remote_copy(
            src_ref=source,
            dst_ref=target,
            send_sem=self.send.at[len(self.sent)],
            recv_sem=self.recv.at[self.number(kind)],
            device_id=device,
            device_id_type=pl.DeviceIdType.MESH,
        )

    def put(self, source, target, kind, device):
        copy = self.copy(source, target, kind, device)
        copy.start()
        self.sent.append(copy)

    def got(self, view, kind):
        pltpu.make_async_remote_copy(
            src_ref=view,
            dst_ref=view,
            send_sem=self.send.at[0],
            recv_sem=self.recv.at[self.number(kind)],
            device_id=self.device("w", "core"),
            device_id_type=pl.DeviceIdType.MESH,
        ).wait_recv()

    def local(self, source, target):
        copy = pltpu.make_async_copy(source, target, self.own_sem.at[len(self.locals)])
        copy.start()
        self.locals.append(copy)


def attention_kernel(
    hidden, modulation, w_query, w_key, w_value, q_gain, k_gain, positions, segs, rates,
    attended, keys_all, values_all,
    hidden_all, modulated, weights, raw, key_own, value_own, squares, tables,
    query_own, marks, key_buf, value_buf, top, acc,
    send, recv, own_sem, load_sem,
):
    net = Net(send, recv, own_sem)
    rows, width = hidden.shape
    deep = w_query.shape[0]
    features = modulation.shape[1]
    heads = width // HEAD_DIM

    barrier = pltpu.get_barrier_semaphore()
    partners = net.partners()
    for device in partners:
        pl.semaphore_signal(
            barrier, inc=1, device_id=device, device_id_type=pl.DeviceIdType.MESH
        )
    pl.semaphore_wait(barrier, len(partners))

    def cut(start, size, half):
        if half is None:
            return pl.ds(pl.multiple_of(start, 16), size)
        return pl.ds(pl.multiple_of(start + half * (size // 2), 16), size // 2)

    def weight_view(which):
        return lambda slot, half: weights.at[which, cut(slot * deep, deep, half)]

    def token_view(ref):
        return lambda slot, half: ref.at[slot, cut(0, ref.shape[1], half)]

    hid = Ring(net, "x", hidden, token_view(hidden_all), True, False)
    wk = Ring(net, "wk", w_key, weight_view(1), True, True)
    wv = Ring(net, "wv", w_value, weight_view(2), False, True)
    wq = Ring(net, "wq", w_query, weight_view(0), True, True)
    kk = Ring(net, "kk", key_own, token_view(keys_all), True, True)
    vv = Ring(net, "vv", value_own, token_view(values_all), False, True)

    def pull(*queues):
        queues = [list(q) for q in queues]
        while any(queues):
            for q in queues:
                if q:
                    q.pop(0)()

    hid.start()
    wv.start()
    wk.start()

    def column(line):
        return jnp.broadcast_to(line, (HEAD_DIM, line.shape[1])).T

    angle = jnp.zeros((rows, HEAD_DIM), jnp.float32)
    for i in range(3):
        angle = angle + column(positions[i : i + 1, :].astype(jnp.float32)) * rates[i : i + 1]
    lane = lax.broadcasted_iota(jnp.int32, angle.shape, 1)
    even = lane % 2 == 0
    tables[0] = jnp.cos(angle)
    sine = jnp.sin(angle)
    tables[1] = jnp.where(even, -sine, sine)

    @pl.loop(0, segs.shape[0])
    def _(i):
        numbers = jnp.broadcast_to(segs[pl.ds(i, 1), :], (HEAD_DIM, HEAD_DIM))
        kinds = lax.broadcasted_iota(jnp.int32, numbers.shape, 0)
        part = pl.ds(pl.multiple_of(i * HEAD_DIM, HEAD_DIM), HEAD_DIM)
        marks[:, part] = jnp.where(numbers == kinds, 0.0, -1.0).astype(jnp.bfloat16)

    def normalise():
        net.locals[0].wait()
        groups = hidden_all.shape[0]

        def add(g, total):
            return total + jnp.sum(hidden_all[g].astype(jnp.float32), axis=1, keepdims=True)

        zero = jnp.zeros((rows, 1), jnp.float32)
        average = lax.fori_loop(0, groups, add, zero) / features

        def spread(g, total):
            centred = hidden_all[g].astype(jnp.float32) - average
            return total + jnp.sum(centred * centred, axis=1, keepdims=True)

        variance = lax.fori_loop(0, groups, spread, zero) / features
        scale = lax.rsqrt(variance + epsilon)

        @pl.loop(0, groups)
        def _(g):
            part = pl.ds(pl.multiple_of(g * width, width), width)
            normed = (hidden_all[g].astype(jnp.float32) - average) * scale
            shifted = normed * (1.0 + modulation[1:2, part]) + modulation[0:1, part]
            modulated[:, part] = shifted.astype(jnp.bfloat16)

    def project(which):
        step = 2 * width
        raw[...] = jnp.zeros_like(raw)

        @pl.loop(0, features // step)
        def _(g):
            part = pl.ds(pl.multiple_of(g * step, step), step)
            raw[...] += jnp.dot(
                modulated[:, part], weights[which, part, :], preferred_element_type=jnp.float32
            )

    def send_squares(number):
        whole = raw[...]
        part = jnp.zeros((rows, HEAD_DIM), jnp.float32)
        for h in range(heads):
            piece = whole[:, h * HEAD_DIM : (h + 1) * HEAD_DIM]
            part = part + piece * piece
        total = jnp.sum(part.T, axis=0, keepdims=True)
        mine = squares.at[number, net.col]
        squares[number, net.col] = jnp.broadcast_to(total, (8, rows))
        for i, device in enumerate(net.peers()):
            net.put(mine, mine, ("sq", number, i), device)

    def turned(number, gain, scale):
        others = [(p, s) for p in (0, 1) for s in range(4) if (p, s) != (0, 0)]
        for i, (pair, step) in enumerate(others):
            net.got(squares.at[number, net.col_at(pair, -step)], ("sq", number, i))
        total = jnp.sum(squares[number], axis=0)
        factor = lax.rsqrt(column(total[0:1]) / features + epsilon) * scale
        made = []
        for h in range(heads):
            normed = raw[:, h * HEAD_DIM : (h + 1) * HEAD_DIM] * factor * gain[h : h + 1, :]
            swapped = jnp.where(
                even, pltpu.roll(normed, HEAD_DIM - 1, 1), pltpu.roll(normed, 1, 1)
            )
            made.append(normed * tables[0] + swapped * tables[1])
        return made

    def loads(chip, slot):
        for i, (source, target) in enumerate(((keys_all, key_buf), (values_all, value_buf))):
            for core in range(2):
                yield pltpu.make_async_copy(
                    source.at[chip * 2 + core],
                    target.at[slot, core],
                    load_sem.at[slot, 2 * i + core],
                )

    ones = jnp.ones((2 * rows, HEAD_DIM), jnp.bfloat16)

    def attend(chip, slot):
        for copy in loads(chip, slot):
            copy.wait()
        chip_start = pl.multiple_of(chip * 2 * rows, HEAD_DIM)
        key_marks = marks[:, pl.ds(chip_start, 2 * rows)]
        for h in range(heads):
            part = slice(h * HEAD_DIM, (h + 1) * HEAD_DIM)
            keys = jnp.concatenate([key_buf[slot, 0, part], key_buf[slot, 1, part]], axis=1)
            scores = jnp.dot(
                query_own[h],
                jnp.concatenate([keys, key_marks], axis=0),
                preferred_element_type=jnp.float32,
            )
            old = top[h]
            new = jnp.maximum(old, jnp.max(scores, axis=1, keepdims=True))
            top[h] = new
            chances = jnp.exp2(scores - new[:, 0:1])
            factor = jnp.exp2(old - new)
            mixed = jnp.dot(
                chances.astype(jnp.bfloat16),
                jnp.concatenate(
                    [value_buf[slot, :, :, part].reshape(2 * rows, HEAD_DIM), ones], axis=1
                ),
                preferred_element_type=jnp.float32,
            )
            acc[h] = acc[h] * jnp.concatenate([factor, factor], axis=1) + mixed

    waiting = []

    def block(pair, step):
        chip = net.row_at(pair, step, False) // 2
        if (pair, step) == (0, 0):
            for copy in net.locals[4:6]:
                copy.wait()
        for ring in (kk, vv):
            ring.met(pair, step)
        slot = block_count[0] % 2
        block_count[0] += 1
        for copy in loads(chip, slot):
            copy.start()
        if waiting:
            attend(*waiting.pop())
        waiting.append((chip, slot))

    block_count = [0]

    v_steps, k_steps, q_steps = wv.events(), wk.events(), wq.events()
    x_steps = hid.events()
    pull(v_steps[:5], k_steps[:5], x_steps[:5])
    wq.start()
    pull(v_steps[5:6], k_steps[5:6], x_steps[5:7])
    normalise()
    pull(v_steps[6:7], k_steps[6:7])
    wv.finish()
    for copy in net.locals[1:3]:
        copy.wait()
    project(2)
    value_own[...] = raw[...].astype(jnp.bfloat16)
    vv.start()
    wk.finish()
    project(1)
    send_squares(0)
    pull(q_steps[:3])
    for h, piece in enumerate(turned(0, k_gain, 1.0)):
        key_own[h * HEAD_DIM : (h + 1) * HEAD_DIM, :] = piece.T.astype(jnp.bfloat16)
    kk.start()
    v_steps, k_steps = vv.events(), kk.events()
    pull(q_steps[3:], v_steps[:3], k_steps[:3])
    wq.finish()
    net.locals[3].wait()
    project(0)
    send_squares(1)
    top[...] = jnp.full_like(top, -1e20)
    acc[...] = jnp.zeros_like(acc)
    pull(v_steps[3:4], k_steps[3:5])
    own_lines = rows // HEAD_DIM
    numbers = jnp.concatenate(
        [
            column(segs[pl.ds(net.row * own_lines + i, 1), :].astype(jnp.float32))
            for i in range(own_lines)
        ],
        axis=0,
    )
    query_marks = jnp.where(numbers == lane.astype(jnp.float32), 1e30, 0.0).astype(jnp.bfloat16)
    for h, piece in enumerate(turned(1, q_gain, HEAD_DIM ** (-0.5) * LOG2E)):
        query_own[h] = jnp.concatenate([piece.astype(jnp.bfloat16), query_marks], axis=1)
    block(0, 0)
    block(0, -1)
    block(0, 1)
    pull(v_steps[4:6], k_steps[5:6])
    block(1, 0)
    block(1, -1)
    block(1, 1)
    block(0, 2)
    attend(*waiting.pop())
    pull(v_steps[6:7], k_steps[6:7])
    block(1, 2)
    attend(*waiting.pop())
    for h in range(heads):
        part = slice(h * HEAD_DIM, (h + 1) * HEAD_DIM)
        attended[:, part] = (acc[h, :, :HEAD_DIM] / acc[h, :, HEAD_DIM:]).astype(attended.dtype)
    for copy in net.sent:
        copy.wait_send()


def pages_kernel(page_table, result, keys, values, attended, pages, turned, sem):
    own_pages = pages.shape[1]
    blocks = keys.shape[2] // PAGE
    first = lax.axis_index("row") * own_pages

    def look(b, found):
        return tuple(
            jnp.where(page_table[b] == first + j, b, found[j]) for j in range(own_pages)
        )

    start = tuple(jnp.int32(0) for _ in range(own_pages))
    found = lax.fori_loop(0, page_table.shape[0], look, start)
    copies = []
    for j in range(own_pages):
        shard = found[j] // blocks
        part = pl.ds(pl.multiple_of((found[j] - shard * blocks) * PAGE, PAGE), PAGE)
        copies.append(
            pltpu.make_async_copy(keys.at[shard, :, part], turned.at[j], sem.at[j])
        )
        copies.append(
            pltpu.make_async_copy(
                values.at[shard, part], pages.at[1, j], sem.at[own_pages + j]
            )
        )
    copies.append(pltpu.make_async_copy(result, attended, sem.at[2 * own_pages]))
    for copy in copies:
        copy.start()
    for j in range(own_pages):
        copies[2 * j].wait()
        pages[0, j] = turned[j].T
    for j in range(own_pages):
        copies[2 * j + 1].wait()
    copies[-1].wait()


def store_pages(page_table, result, keys, values):
    rows, width = result.shape
    any_spec = pl.BlockSpec(memory_space=pl.ANY)
    vmem = pl.BlockSpec(memory_space=pltpu.VMEM)
    own_pages = rows // PAGE
    return pl.pallas_call(
        pages_kernel,
        out_shape=(
            jax.ShapeDtypeStruct((rows, width), jnp.bfloat16),
            jax.ShapeDtypeStruct((2, own_pages, PAGE, width), jnp.bfloat16),
        ),
        in_specs=[pl.BlockSpec(memory_space=pltpu.SMEM), any_spec, any_spec, any_spec],
        out_specs=(vmem, vmem),
        scratch_shapes=[
            pltpu.VMEM((own_pages, width, PAGE), jnp.bfloat16),
            pltpu.SemaphoreType.DMA((2 * own_pages + 1,)),
        ],
        compiler_params=pltpu.CompilerParams(vmem_limit_bytes=60 * 2**20),
        name="pages",
    )(page_table, result, keys, values)


def body(
    hidden, modulation, w_query, w_key, w_value, q_gain, k_gain, positions, segment_ids, page_table
):
    rows, width = hidden.shape
    deep = w_query.shape[0]
    features = modulation.shape[1]
    tokens = segment_ids.shape[0]
    members, groups, heads = features // deep, features // width, width // HEAD_DIM
    any_spec = pl.BlockSpec(memory_space=pl.ANY)
    vmem = pl.BlockSpec(memory_space=pltpu.VMEM)
    key_shards = jax.ShapeDtypeStruct((members, width, rows), jnp.bfloat16)
    value_shards = jax.ShapeDtypeStruct((members, rows, width), jnp.bfloat16)
    attended, keys, values = pl.pallas_call(
        attention_kernel,
        out_shape=(
            jax.ShapeDtypeStruct((rows, width), jnp.bfloat16), key_shards, value_shards
        ),
        in_specs=[any_spec, vmem, any_spec, any_spec, any_spec, vmem, vmem, vmem, vmem, vmem],
        out_specs=(vmem, any_spec, any_spec),
        scratch_shapes=[
            pltpu.VMEM((groups, rows, width), jnp.bfloat16),
            pltpu.VMEM((rows, features), jnp.bfloat16),
            pltpu.VMEM((3, features, width), jnp.bfloat16),
            pltpu.VMEM((rows, width), jnp.float32),
            pltpu.VMEM((width, rows), jnp.bfloat16),
            pltpu.VMEM((rows, width), jnp.bfloat16),
            pltpu.VMEM((2, groups, 8, rows), jnp.float32),
            pltpu.VMEM((2, rows, HEAD_DIM), jnp.float32),
            pltpu.VMEM((heads, rows, 2 * HEAD_DIM), jnp.bfloat16),
            pltpu.VMEM((HEAD_DIM, tokens), jnp.bfloat16),
            pltpu.VMEM((2, 2, width, rows), jnp.bfloat16),
            pltpu.VMEM((2, 2, rows, width), jnp.bfloat16),
            pltpu.VMEM((heads, rows, HEAD_DIM), jnp.float32),
            pltpu.VMEM((heads, rows, 2 * HEAD_DIM), jnp.float32),
            pltpu.SemaphoreType.DMA((128,)),
            pltpu.SemaphoreType.DMA((128,)),
            pltpu.SemaphoreType.DMA((6,)),
            pltpu.SemaphoreType.DMA((2, 4)),
        ],
        compiler_params=pltpu.CompilerParams(
            collective_id=0, has_side_effects=True, vmem_limit_bytes=58 * 2**20
        ),
        name="attention",
    )(
        hidden, modulation, w_query, w_key, w_value,
        q_gain.reshape(heads, HEAD_DIM), k_gain.reshape(heads, HEAD_DIM), positions,
        segment_ids.reshape(tokens // HEAD_DIM, HEAD_DIM),
        jnp.asarray(rotary_rates(HEAD_DIM // 2)),
    )
    return store_pages(page_table, attended, keys, values)


def solution(mesh):
    in_specs = (
        P("row", "col"),
        P(),
        P("row", "col"),
        P("row", "col"),
        P("row", "col"),
        P("col"),
        P("col"),
        P(None, "row"),
        P(),
        P(),
    )
    out_specs = (P("row", "col"), P(None, "row", None, "col"))
    return jax.shard_map(body, mesh=mesh, in_specs=in_specs, out_specs=out_specs, check_vma=False)
```
